32 devices in a mesh: gx: 8 (over z, y), gy: 2 (over core), gz: 2 (over x).
Axes of the slice: x: 2, y: 2, z: 4, core: 2. Of those that a mesh axis runs over, the one named last changes fastest.
Arguments:
- conserved: bfloat16 [5, 64, 16, 256], P(None, 'gx', 'gy', 'gz'), may hold values from -0.5 to 5, as said below
- sigma_prev: float32 [64, 16, 256], P('gx', 'gy', 'gz'), may hold values from -6 to 6
Outputs:
- new_state: float32 [5, 64, 16, 256], P(None, 'gx', 'gy', 'gz')
- entropic: float32 [64, 16, 256], P('gx', 'gy', 'gz')
The draws below stay inside these ranges and needn't reach their ends.
Inputs may be any that keep to these rules, and one draw needn't show every extreme that they name: `conserved`: field 0 (density) lies in 0.5 to 2, fields 1 to 3 (momenta) in -0.5 to 0.5, field 4 (total energy) in 2 to 5.
All inputs are finite; a program needn't handle non-finite values.
Results may differ from the reference program's by a relative error of at most 0.0013.
Values may be sent and summed in bfloat16 or wider, within the bound.
A program may use at most 64 MiB of HBM per device.

```python
import jax
import jax.numpy as jnp
from jax import lax

SWEEPS = 4
NX = 64
NY = 16
NZ = 256


def draw_conserved(key, part):
    subkeys = jax.random.split(jax.random.fold_in(key, 17), 3)
    grid_shape = (NX, NY, NZ)
    rough_density = jax.random.uniform(subkeys[0], grid_shape, jnp.float32)
    rough_energy = jax.random.uniform(subkeys[2], grid_shape, jnp.float32)
    momentum = jax.random.uniform(subkeys[1], (3,) + grid_shape, jnp.float32, -0.5, 0.5)
    density = 0.5 + 1.5 * rough_density
    energy = 2.0 + 3.0 * rough_energy
    stacked = jnp.concatenate([density[None], momentum, energy[None]], axis=0)
    return stacked.astype(jnp.bfloat16)


def level_of(rng, shape, cuts, low, largest):
    gain, own = 1.0, jax.random.fold_in(rng, 6)
    for dim, parts in cuts:
        draws = jnp.exp(jax.random.uniform(jax.random.fold_in(own, dim), (parts,), jnp.float32, low / len(cuts), largest / len(cuts)))
        gain = gain * jnp.repeat(draws, shape[dim] // parts).reshape([-1 if axis == dim else 1 for axis in range(len(shape))])
    return gain


def centred(stream_key, extent, width, most, pieces=(), kind=jnp.bfloat16):
    drawn = jax.random.normal(stream_key, extent, jnp.float32) * width
    if len(pieces) > 0:
        drawn = level_of(stream_key, extent, pieces, -0.22, 0.18) * drawn
    return jnp.clip(drawn, min=-most, max=most).astype(kind)


def setup_inputs(seed: int = 0) -> dict:
    arg_keys = jax.random.split(jax.random.key(seed), 3)
    conserved = draw_conserved(jax.random.fold_in(arg_keys[2], 71), 0)
    sigma_prev = centred(arg_keys[1], (NX, NY, NZ), 1.0, 6.0, ((0, 8), (1, 2), (2, 2)), jnp.float32)
    return {"conserved": conserved, "sigma_prev": sigma_prev}


gamma_gas = 1.4
alpha_reg = 4.0
time_step = 0.08

def crop(tensor, margin):
    return tensor[..., margin:tensor.shape[-3] - margin, margin:tensor.shape[-2] - margin, margin:tensor.shape[-1] - margin]

def cut_axis(tensor, axis_dim, start, length):
    return lax.slice_in_dim(tensor, start, start + length, axis=axis_dim)

def trim_except(tensor, keep_axis, margin):
    for spatial in range(3):
        if spatial != keep_axis:
            axis_dim = tensor.ndim - 3 + spatial
            tensor = cut_axis(tensor, axis_dim, margin, tensor.shape[axis_dim] - 2 * margin)
    return tensor

def central(tensor, spatial):
    axis_dim = tensor.ndim - 3 + spatial
    length = tensor.shape[axis_dim] - 2
    return 0.5 * (cut_axis(tensor, axis_dim, 2, length) - cut_axis(tensor, axis_dim, 0, length))

def stencil(padded):
    center = padded[1:-1, 1:-1, 1:-1]
    beside_all = [padded[2:, 1:-1, 1:-1], padded[:-2, 1:-1, 1:-1], padded[1:-1, 2:, 1:-1], padded[1:-1, :-2, 1:-1], padded[1:-1, 1:-1, 2:], padded[1:-1, 1:-1, :-2]]
    return (center, beside_all)

def sweep(sigma_pad, inverse_pad, source):
    sigma_mid, sigma_around = stencil(sigma_pad)
    inverse_mid, inverse_around = stencil(inverse_pad)
    numerator = source
    denominator = inverse_mid
    for neighbor_sigma, neighbor_inverse in zip(sigma_around, inverse_around):
        weight = alpha_reg * 0.5 * (inverse_mid + neighbor_inverse)
        numerator = numerator + weight * neighbor_sigma
        denominator = denominator + weight
    return numerator / denominator

def entropic_source(halo_state, margin):
    region = crop(halo_state, 2 - margin)
    velocity = region[1:4] / region[0]
    gradient = [trim_except(central(velocity, spatial), spatial, 1) for spatial in range(3)]
    divergence = gradient[0][0] + gradient[1][1] + gradient[2][2]
    product = divergence * divergence
    for first in range(3):
        for second in range(3):
            product = product + gradient[first][second] * gradient[second][first]
    return alpha_reg * product

def physical_flux(values, spatial):
    density = values[0]
    velocity = values[1:4] / density
    kinetic = 0.5 * (values[1] * velocity[0] + values[2] * velocity[1] + values[3] * velocity[2])
    pressure = (gamma_gas - 1.0) * (values[4] - kinetic)
    normal = velocity[spatial]
    momentum = [values[1 + component] * normal for component in range(3)]
    momentum[spatial] = momentum[spatial] + pressure
    flux_vec = jnp.stack([values[1 + spatial]] + momentum + [(values[4] + pressure) * normal])
    wave_speed = jnp.abs(normal) + jnp.sqrt(gamma_gas * jnp.abs(pressure) / density)
    return (flux_vec, wave_speed)

def flux_divergence(halo_state, sigma_pad):
    summed = None
    for spatial in range(3):
        pencil = trim_except(halo_state, spatial, 3)
        axis_dim = spatial + 1
        face_count = pencil.shape[axis_dim] - 5
        shifted = [cut_axis(pencil, axis_dim, offset, face_count) for offset in range(6)]
        left_state = (2.0 * shifted[0] - 13.0 * shifted[1] + 47.0 * shifted[2] + 27.0 * shifted[3] - 3.0 * shifted[4]) / 60.0
        right_state = (2.0 * shifted[5] - 13.0 * shifted[4] + 47.0 * shifted[3] + 27.0 * shifted[2] - 3.0 * shifted[1]) / 60.0
        flux_left, speed_left = physical_flux(left_state, spatial)
        flux_right, speed_right = physical_flux(right_state, spatial)
        numeric = 0.5 * (flux_left + flux_right) - 0.5 * jnp.maximum(speed_left, speed_right) * (right_state - left_state)
        change = cut_axis(numeric, axis_dim, 1, face_count - 1) - cut_axis(numeric, axis_dim, 0, face_count - 1)
        sigma_line = trim_except(sigma_pad, spatial, 1)
        grad_sigma = central(sigma_line, spatial)
        vel_line = cut_axis(pencil, axis_dim, 2, face_count + 1)
        vel_normal = vel_line[1 + spatial] / vel_line[0]
        power_term = central(sigma_line * vel_normal, spatial)
        update = [change[index] for index in range(5)]
        update[1 + spatial] = update[1 + spatial] + grad_sigma
        update[4] = update[4] + power_term
        increment = jnp.stack(update)
        summed = increment if summed is None else summed + increment
    return -summed

def wrap_pad(tensor, depth_cells):
    widths = [(0, 0)] * (tensor.ndim - 3) + [(depth_cells, depth_cells)] * 3
    return jnp.pad(tensor, widths, mode='wrap')

def reference(conserved, sigma_prev):
    initial = conserved.astype(jnp.float32)
    section_state = conserved
    entropic = sigma_prev
    new_state = initial
    for section_index in range(2):
        halo_state = wrap_pad(section_state, 3).astype(jnp.float32)
        source = entropic_source(halo_state, 0)
        inverse = crop(1.0 / halo_state[0], 2)
        for sweep_index in range(SWEEPS):
            entropic = sweep(wrap_pad(entropic, 1), inverse, source)
        tendency = flux_divergence(halo_state, wrap_pad(entropic, 1))
        if section_index == 0:
            section_state = (initial + time_step * tendency).astype(jnp.bfloat16)
        else:
            new_state = 0.5 * (initial + section_state.astype(jnp.float32) + time_step * tendency)
    return (new_state, entropic)
```

```python
import functools

import jax
import jax.numpy as jnp
from jax import lax
from jax.experimental import pallas as pl
from jax.experimental.pallas import tpu as pltpu
from jax.sharding import PartitionSpec as P

SWEEPS = 4
HALO = SWEEPS + 1
REACH = 3
gamma_gas = 1.4
alpha_reg = 4.0
time_step = 0.08
MESH = pl.DeviceIdType.MESH
F32 = jnp.float32
BF16 = jnp.bfloat16

SIG, EN = 4, 5
FIRST_COPIES, SECOND_COPIES = 17, 8
G_SIB, G_OUT, G_FAR, G_ZSAME, G_ZSIB, G_ZOUT = range(6)


def edges(c, p1, m1, p2, m2):
    even = (47.0 / 60.0) * c + (7.0 / 60.0) * (p1 + m1) - (0.5 / 60.0) * (p2 + m2)
    odd = (20.0 / 60.0) * (p1 - m1) - (2.5 / 60.0) * (p2 - m2)
    return even + odd, even - odd


def physical_flux(v, d):
    inv = 1.0 / v[0]
    u = [v[1] * inv, v[2] * inv, v[3] * inv]
    kinetic = 0.5 * (v[1] * u[0] + v[2] * u[1] + v[3] * u[2])
    p = (gamma_gas - 1.0) * (v[4] - kinetic)
    n = u[d]
    flux = [v[1 + d], v[1] * n, v[2] * n, v[3] * n, (v[4] + p) * n]
    flux[1 + d] = flux[1 + d] + p
    return flux, jnp.abs(n) + jnp.sqrt(gamma_gas * jnp.abs(p) * inv)


def face_flux(left, right, d):
    fl, sl = physical_flux(left, d)
    fr, sr = physical_flux(right, d)
    speed = jnp.maximum(sl, sr)
    return [0.5 * ((a + b) - speed * (r - l)) for a, b, l, r in zip(fl, fr, left, right)]


def up(v, axis, by=1):
    return pltpu.roll(v, (v.shape[axis] - by) % v.shape[axis], axis)


def down(v, axis, by=1):
    return pltpu.roll(v, by, axis)


def kernel(counts, cons, sigma, new_out, ent_out, SGB, FP, R, ZR, STO, STS, PKS, PKO, FO, FE,
           QF, CI, U, INV, CO, SA, SB, WQ, WU, WI, WC, WS, ZB, T, send_sem, recv_sem, last_sem):
    gx, h, gz = lax.axis_index("gx"), lax.axis_index("gy"), lax.axis_index("gz")
    nx, ny, nz = sigma.shape
    m = nx // 2
    np_ = m + 2 * HALO
    own0, sib0, end = HALO, HALO + m, HALO + 2 * m
    slot = nz // nx
    half = slot // 2
    near_rows, far_rows = slice(0, ny), slice(ny, 2 * ny)
    sg = (1 - 2 * h).astype(F32)

    right, left = lax.rem(gx + 1, counts[0]), lax.rem(gx + counts[0] - 1, counts[0])
    outer = lax.rem(gx + counts[0] - 1 + 2 * h, counts[0])
    inner = lax.rem(gx + counts[0] + 1 - 2 * h, counts[0])
    oz = 1 - gz
    rows_of = (h * 0, h * 0 + 1)

    def frame(e):
        return e + h * (np_ - 1 - 2 * e)

    def block(k):
        return k + h * (nx - 1 - 2 * k)

    lane = lax.broadcasted_iota(jnp.int32, (ny, nz), 1)
    lane2 = lax.broadcasted_iota(jnp.int32, (2 * ny, nz), 1)
    lower2 = (lane2 & (slot - 1)) < half
    first2 = lane2 < nz // 2

    def strips(parts, lanes):
        acc = None
        for at, v in parts:
            r = pltpu.roll(v, (half + slot * at) % nz, 1)
            acc = r if acc is None else jnp.where(lanes >= slot * at, r, acc)
        return acc

    def descriptors(listed, base):
        made = []
        for n, (sec, src, dst, group, where) in enumerate(listed):
            made.append(pltpu.make_async_remote_copy(
                src_ref=src, dst_ref=dst, send_sem=send_sem.at[base + n],
                recv_sem=recv_sem.at[sec, group], device_id=where, device_id_type=MESH,
            ))
        return made

    def arrived(sec, group, ref):
        pltpu.make_async_remote_copy(
            src_ref=ref, dst_ref=ref, send_sem=send_sem.at[0], recv_sem=recv_sem.at[sec, group],
            device_id=(gx, 1 - h, gz), device_id_type=MESH,
        ).wait_recv()

    barrier = pltpu.get_barrier_semaphore()
    peers = [(gx, 1 - h, gz), (outer, h, oz), (outer, 1 - h, oz)]
    peers += [(x, y, gz) for x in (right, left) for y in (h, 1 - h)]
    peers += [(gx, h, oz), (gx, 1 - h, oz)]
    for peer in peers:
        pl.semaphore_signal(barrier, inc=1, device_id=peer, device_id_type=MESH)

    SGB[...] = sigma[...].astype(BF16)
    for f in range(6):
        for target in (0, 1):
            parts = []
            for k in range(nx):
                p = k if target == 0 else nx - 1 - k
                parts.append((k, sigma[p] if f == SIG else cons[min(f, 4), p].astype(F32)))
            FP[target, f] = strips(parts, lane).astype(BF16)

    pl.semaphore_wait(barrier, len(peers))

    def first_sends():
        listed = []

        def copy(*c):
            listed.append(c)

        for to, target, a, e, hf in ((right, 0, nx - HALO, 0, h), (left, 1, 0, sib0, 1 - h)):
            copy(0, cons.at[0:4, a:a + HALO], R.at[0, hf, 0:4, e:e + HALO], G_OUT, (to, rows_of[target], gz))
            copy(0, SGB.at[a:a + HALO], R.at[0, hf, SIG, e:e + HALO], G_OUT, (to, rows_of[target], gz))
            skip = HALO - REACH if target == 0 else 0
            copy(0, cons.at[4, a + skip:a + skip + REACH],
                 R.at[0, hf, EN, e + skip:e + skip + REACH], G_OUT, (to, rows_of[target], gz))
        for to, target, a, e, hf in ((right, 1, nx - 1, 0, 1 - h), (left, 0, 0, np_ - 1, h)):
            copy(0, cons.at[0:4, a:a + 1], R.at[0, hf, 0:4, e:e + 1], G_FAR, (to, rows_of[target], gz))
            copy(0, SGB.at[a:a + 1], R.at[0, hf, SIG, e:e + 1], G_FAR, (to, rows_of[target], gz))
        for target, hf in ((0, h), (1, 1 - h)):
            copy(0, FP.at[target], ZR.at[0, 0, hf], G_ZSAME, (gx, rows_of[target], oz))
            to = right if target == 0 else left
            copy(0, FP.at[target, 0:EN], ZR.at[0, 2, hf, 0:EN], G_ZOUT, (to, rows_of[target], oz))
        e = HALO - m + m * h
        sib = (gx, 1 - h, gz)
        copy(0, cons.at[0:4], R.at[0, 1, 0:4, pl.ds(e, nx)], G_SIB, sib)
        copy(0, SGB, R.at[0, 1, SIG, pl.ds(e, nx)], G_SIB, sib)
        copy(0, cons.at[4], R.at[0, 1, EN, pl.ds(e, nx)], G_SIB, sib)

        return descriptors(listed, 0)

    def second_sends():
        listed = []

        def copy(*c):
            listed.append(c)

        e = sib0 - 2 * m * h
        to = (outer, 1 - h, gz)
        copy(1, STO.at[:, 0:EN], R.at[1, :, 0:EN, pl.ds(e, m)], G_OUT, to)
        copy(1, STO.at[:, EN, pl.ds(h, REACH)], R.at[1, :, EN, pl.ds(e + h, REACH)], G_OUT, to)
        copy(1, STS.at[:, :, 1:2], R.at[1, :, 0:EN, pl.ds((np_ - 1) * h, 1)], G_OUT, (inner, h, gz))
        copy(1, STS.at[:, :, 0:1], R.at[1, :, 0:EN, pl.ds((np_ - 1) * (1 - h), 1)], G_FAR,
             (outer, h, gz))
        e = HALO - m + 2 * m * h
        copy(1, STO, R.at[1, :, :, pl.ds(e, m)], G_SIB, (gx, 1 - h, gz))
        copy(1, PKS, ZR.at[1, 0], G_ZSAME, (gx, h, oz))
        copy(1, PKO, ZR.at[1, 1, :, 0:EN], G_ZSIB, (gx, 1 - h, oz))
        copy(1, PKO, ZR.at[1, 2, :, 0:EN], G_ZOUT, (outer, 1 - h, oz))
        return descriptors(listed, FIRST_COPIES)

    first = first_sends()
    for c in first:
        c.start()

    for k in range(nx):
        p = block(k)
        for f in range(5):
            v = cons.at[f][p].astype(F32)
            QF[f, own0 + k, near_rows] = v * sg if f == 1 else v
        SA[own0 + k, near_rows] = sigma[p]

    def take(sec, e, halves, fields=6):
        for hf in halves:
            rows = far_rows if hf else near_rows
            for f in range(fields):
                v = R[sec, hf, f, frame(e)].astype(F32)
                if f == SIG:
                    SA[e, rows] = v
                else:
                    QF[min(f, 4), e, rows] = v * sg if f == 1 else v

    def line_flux(fields, d, axis):
        lefts, rights = [], []
        for c in fields:
            l, r = edges(c, up(c, axis), down(c, axis), up(c, axis, 2), down(c, axis, 2))
            lefts.append(l)
            rights.append(up(r, axis))
        return [v - down(v, axis) for v in face_flux(lefts, rights, d)]

    def x_face(p):
        lefts, rights = [], []
        for f in range(5):
            v = [QF[f, p + o] for o in range(-2, 4)]
            lefts.append(edges(v[2], v[3], v[1], v[4], v[0])[0])
            rights.append(edges(v[3], v[4], v[2], v[5], v[1])[1])
        return face_flux(lefts, rights, 0)

    def velocities(p):
        inv = 1.0 / QF[0, p]
        INV[p] = inv
        for a in range(3):
            U[a, p] = QF[1 + a, p] * inv

    def stencil_terms(g, c, around):
        div = g[0][0] + g[1][1] + g[2][2]
        total = div * div + g[0][0] * g[0][0] + g[1][1] * g[1][1] + g[2][2] * g[2][2]
        total = total + 2.0 * (g[0][1] * g[1][0] + g[0][2] * g[2][0] + g[1][2] * g[2][1])
        source = (alpha_reg * 0.25) * total
        w = [(alpha_reg * 0.5) * (c + n) for n in around]
        scale = 1.0 / (c + ((w[0] + w[1]) + (w[2] + w[3]) + (w[4] + w[5])))
        return [v * scale for v in w] + [source * scale]

    def coefficients(p):
        g = []
        for a in range(3):
            u = U[a, p]
            g.append([
                U[a, p + 1] - U[a, p - 1], up(u, 0) - down(u, 0), up(u, 1) - down(u, 1),
            ])
        c = INV[p]
        around = [INV[p + 1], INV[p - 1], up(c, 0), down(c, 0), up(c, 1), down(c, 1)]
        for n, v in enumerate(stencil_terms(g, c, around)):
            CO[n, p] = v

    def jacobi(co, c, xp, xm):
        out = co(6) + co(0) * xp + co(1) * xm
        out = out + (co(2) * up(c, 0) + co(3) * down(c, 0))
        return out + (co(4) * up(c, 1) + co(5) * down(c, 1))

    def main_sweep(step, planes):
        read, write = (SA, SB) if step % 2 == 0 else (SB, SA)
        for p in planes:
            write[p] = jacobi(lambda n: CO[n, p], read[p], read[p + 1], read[p - 1])

    early = [range(own0 + 1 + t, end - 1 - t) for t in range(SWEEPS)]
    near = jnp.logical_or(lane2 < REACH, lane2 >= nz - REACH)
    edge = jnp.logical_or(lane2 < SWEEPS, lane2 >= nz - SWEEPS)
    ends = jnp.logical_or(lane2 == 0, lane2 == nz - 1)

    def ring_next(a, b):
        ua, ub = up(a, 1, slot), up(b, 1, slot)
        cut = lane2 >= nz - slot
        return jnp.where(cut, ub, ua), jnp.where(cut, ua, ub)

    def ring_prev(a, b):
        da, db = down(a, 1, slot), down(b, 1, slot)
        cut = lane2 < slot
        return jnp.where(cut, db, da), jnp.where(cut, da, db)

    def joined(own, far):
        return jnp.where(lower2, far, own), jnp.where(lower2, own, far)

    def far_strip(sec, which, f):
        v = jnp.concatenate([ZR[sec, which, hf, f].astype(F32) for hf in (0, 1)], axis=0)
        return v * sg if f == 1 else v

    def local_strip(f, planes):
        src = SA if f == SIG else QF.at[min(f, 4)]
        return strips([(at, src[p]) for at, p in planes], lane2)

    inside = [(k, own0 + k) for k in range(nx)]
    outside = [(0, end)] + [(nx - HALO + e, e) for e in range(HALO)]

    def section(sec, carry):
        arrived(sec, G_SIB, R.at[sec, :, :, 0:m])

        @pl.when(sec == 0)
        def _():
            for e in range(own0, end):
                take(0, e, (1,))

        @pl.when(sec == 1)
        def _():
            for e in range(sib0, end):
                take(1, e, (0, 1))

        for k in range(m):
            p = own0 + k
            c = [QF[f, p] for f in range(5)]
            ychange = line_flux(c, 1, 0)
            zchange = line_flux(c, 2, 1)
            for f in range(5):
                T[f, k] = ychange[f] + jnp.where(near, 0.0, zchange[f])
        h8, h7 = x_face(sib0 - 1), x_face(sib0 - 2)
        for f in range(5):
            T[f, m - 1] = T[f, m - 1] + (h8[f] - h7[f])
            T[f, m - 2] = T[f, m - 2] + h7[f]
        for p in range(own0, end):
            velocities(p)
        for p in early[0]:
            coefficients(p)
        WS[...] = local_strip(SIG, inside)
        for step in range(SWEEPS):
            main_sweep(step, early[step])

        arrived(sec, G_ZSAME, ZR.at[sec, 0])

        @pl.when(sec == 1)
        def _():
            arrived(sec, G_ZSIB, ZR.at[sec, 1, :, 0:EN])

        for f in (0, 1, 2, 3, EN):
            a = far_strip(sec, 0, f)
            if f != EN:
                a = jnp.where(first2, a, far_strip(sec, sec, f))
            WQ[min(f, 4), 0], WQ[min(f, 4), 1] = joined(local_strip(f, inside), a)
        lo = line_flux([WQ[f, 0] for f in range(5)], 2, 1)
        hi = line_flux([WQ[f, 1] for f in range(5)], 2, 1)
        for f in range(5):
            zb = jnp.where(lower2, hi[f], lo[f])
            for k in range(m):
                r = pltpu.roll(zb, nz - half - slot * k, 1)
                T[f, k] = T[f, k] + jnp.where(near, r, 0.0)

        arrived(sec, G_OUT, R.at[sec, :, 0:4, 0:7])
        arrived(sec, G_FAR, R.at[sec, :, 0:EN, 0:1])
        for e in range(HALO):
            take(sec, e, (0, 1), 6 if e >= HALO - REACH else 5)
        take(sec, end, (0, 1), 5)
        faces = [x_face(p) for p in range(own0 - 1, sib0 - 2)]
        for f in range(5):
            for k in range(m - 2):
                T[f, k] = T[f, k] + (faces[k + 1][f] - faces[k][f])
            T[f, m - 2] = T[f, m - 2] - faces[m - 2][f]
        for p in list(range(HALO)) + [end]:
            velocities(p)
        for p in range(1, np_ - 1):
            if p not in early[0]:
                coefficients(p)

        arrived(sec, G_ZOUT, ZR.at[sec, 2, :, 0:EN])
        for f in range(4):
            WQ[f, 2], WQ[f, 3] = joined(local_strip(f, outside), far_strip(sec, 2, f))
        for n in range(4):
            inv = 1.0 / WQ[0, n]
            WI[n] = inv
            for a in range(3):
                WU[a, n] = WQ[1 + a, n] * inv
        a = jnp.where(first2, far_strip(sec, 0, SIG), far_strip(sec, sec, SIG))
        w = list(joined(WS[...], a))
        w += joined(local_strip(SIG, outside), far_strip(sec, 2, SIG))

        for b in (0, 1):
            pair = (b, 2 + b)
            g = [[], []]
            for a in range(3):
                v = [WU[a, n] for n in pair]
                nxt, prv = ring_next(*v), ring_prev(*v)
                for i in (0, 1):
                    g[i].append([nxt[i] - prv[i], up(v[i], 0) - down(v[i], 0),
                                 up(v[i], 1) - down(v[i], 1)])
            c = [WI[n] for n in pair]
            nxt, prv = ring_next(*c), ring_prev(*c)
            for i in (0, 1):
                around = [nxt[i], prv[i], up(c[i], 0), down(c[i], 0), up(c[i], 1), down(c[i], 1)]
                for n, v in enumerate(stencil_terms(g[i], c[i], around)):
                    WC[n, pair[i]] = v

        for step in range(SWEEPS):
            main_sweep(step, [p for p in range(step + 1, np_ - 1 - step) if p not in early[step]])
            fresh = [None] * 4
            for b in (0, 1):
                pair = (b, 2 + b)
                v = [w[n] for n in pair]
                nxt, prv = ring_next(*v), ring_prev(*v)
                for i in (0, 1):
                    fresh[pair[i]] = jacobi(lambda n: WC[n, pair[i]], v[i], nxt[i], prv[i])
            w = fresh
        S = SA

        for g, planes in ((0, [(k, own0 + k) for k in range(m + 1)]), (1, [(nx - 1, own0 - 1)])):
            both = jnp.where(lower2, w[2 * g + 1], w[2 * g])
            for at, p in planes:
                S[p] = jnp.where(edge, pltpu.roll(both, nz - half - slot * at, 1), S[p])
        diffs = []
        for n in (0, 1):
            v = w[n]
            e = v * WU[2, n]
            diffs.append((up(v, 1) - down(v, 1), up(e, 1) - down(e, 1)))
        for i in (0, 1):
            ZB[i] = jnp.where(lower2, diffs[1][i], diffs[0][i])

        for k in range(m):
            p = own0 + k
            shift = nz - half - slot * k
            xp, xm = S[p + 1], S[p - 1]
            T[1, k] = T[1, k] + 0.5 * (xp - xm)
            power = xp * U[0, p + 1] - xm * U[0, p - 1]
            s = S[p]
            T[2, k] = T[2, k] + 0.5 * (up(s, 0) - down(s, 0))
            e = s * U[1, p]
            power = power + (up(e, 0) - down(e, 0))
            T[3, k] = T[3, k] + 0.5 * jnp.where(
                ends, pltpu.roll(ZB[0], shift, 1), up(s, 1) - down(s, 1))
            e = s * U[2, p]
            power = power + jnp.where(ends, pltpu.roll(ZB[1], shift, 1), up(e, 1) - down(e, 1))
            T[4, k] = T[4, k] + 0.5 * power

        @pl.when(sec == 0)
        def _():
            for k in range(m):
                rk = k + h * (m - 1 - 2 * k)
                for f in range(6):
                    if f == SIG:
                        state = S[own0 + k].astype(BF16)
                    else:
                        q = min(f, 4)
                        initial = QF[q, own0 + k]
                        CI[q, k] = initial
                        state = (initial - time_step * T[q, k]).astype(BF16)
                        QF[q, own0 + k] = state.astype(F32)
                        if f == 1:
                            state = (state.astype(F32) * sg).astype(BF16)
                    STO[0, f, rk], STO[1, f, rk] = state[far_rows], state[near_rows]
                    if f != EN and k in (0, m - 1):
                        at = 0 if k == 0 else 1
                        STS[0, f, at], STS[1, f, at] = state[near_rows], state[far_rows]
            order = list(range(m)) + list(range(m - 1, -1, -1))
            for f in range(6):
                src = S if f == SIG else QF.at[min(f, 4)]
                v = strips([(at, src[own0 + k]) for at, k in enumerate(order)], lane2)
                v = (v * sg if f == 1 else v).astype(BF16)
                PKS[0, f], PKS[1, f] = v[near_rows], v[far_rows]
                if f != EN:
                    PKO[0, f], PKO[1, f] = v[far_rows], v[near_rows]
            for c in second_sends():
                c.start()

        @pl.when(sec == 1)
        def _():
            for k in range(m):
                rk = k + h * (m - 1 - 2 * k)
                for f in range(5):
                    v = 0.5 * ((CI[f, k] - time_step * T[f, k]) + QF[f, own0 + k])
                    v = v * sg if f == 1 else v
                    new_out[f, block(k)] = v[near_rows]
                    FO[f, rk] = v[far_rows]
                s = S[own0 + k]
                ent_out[block(k)] = s[near_rows]
                FE[rk] = s[far_rows]

        return carry

    lax.fori_loop(0, 2, section, 0)

    last = []
    for n, (src, dst) in enumerate((
            (FO, new_out.at[:, pl.ds(m * h, m)]), (FE, ent_out.at[pl.ds(m * h, m)]))):
        c = pltpu.make_async_remote_copy(
            src_ref=src, dst_ref=dst, send_sem=last_sem.at[2 * n], recv_sem=last_sem.at[2 * n + 1],
            device_id=(gx, 1 - h, gz), device_id_type=MESH,
        )
        c.start()
        last.append(c)
    for c in first + second_sends():
        c.wait_send()
    for c in last:
        c.wait()


def solution(mesh):
    counts = (mesh.shape["gx"], mesh.shape["gy"], mesh.shape["gz"])
    assert counts[1] == 2 and counts[2] == 2 and counts[0] > 2

    def step(conserved, sigma_prev):
        _, nx, ny, nz = conserved.shape
        m = nx // 2
        np_ = m + 2 * HALO
        wide = (2 * ny, nz)
        slot = nz // nx
        assert nx == 2 * m and HALO == m + 1 and SWEEPS % 2 == 0 and nx * slot == nz
        assert slot >= 4 * SWEEPS and slot & (slot - 1) == 0
        vmem = pl.BlockSpec(memory_space=pltpu.VMEM)
        tile = (ny, nz)
        return pl.pallas_call(
            functools.partial(kernel, counts),
            out_shape=(
                pltpu.VMEM((5, nx, ny, nz), F32),
                pltpu.VMEM((nx, ny, nz), F32),
            ),
            in_specs=[vmem, vmem],
            out_specs=(vmem, vmem),
            scratch_shapes=[
                pltpu.VMEM((nx,) + tile, BF16),
                pltpu.VMEM((2, 6) + tile, BF16),
                pltpu.VMEM((2, 2, 6, np_) + tile, BF16),
                pltpu.VMEM((2, 3, 2, 6) + tile, BF16),
                pltpu.VMEM((2, 6, m) + tile, BF16),
                pltpu.VMEM((2, 5, 2) + tile, BF16),
                pltpu.VMEM((2, 6) + tile, BF16),
                pltpu.VMEM((2, 5) + tile, BF16),
                pltpu.VMEM((5, m) + tile, F32),
                pltpu.VMEM((m,) + tile, F32),
                pltpu.VMEM((5, np_) + wide, F32),
                pltpu.VMEM((5, m) + wide, F32),
                pltpu.VMEM((3, np_) + wide, F32),
                pltpu.VMEM((np_,) + wide, F32),
                pltpu.VMEM((7, np_) + wide, F32),
                pltpu.VMEM((np_,) + wide, F32),
                pltpu.VMEM((np_,) + wide, F32),
                pltpu.VMEM((5, 4) + wide, F32),
                pltpu.VMEM((3, 4) + wide, F32),
                pltpu.VMEM((4,) + wide, F32),
                pltpu.VMEM((7, 4) + wide, F32),
                pltpu.VMEM(wide, F32),
                pltpu.VMEM((2,) + wide, F32),
                pltpu.VMEM((5, m) + wide, F32),
                pltpu.SemaphoreType.DMA((FIRST_COPIES + SECOND_COPIES,)),
                pltpu.SemaphoreType.DMA((2, 6)),
                pltpu.SemaphoreType.DMA((4,)),
            ],
            compiler_params=pltpu.CompilerParams(collective_id=0, has_side_effects=True),
        )(conserved, sigma_prev)

    return jax.shard_map(
        step,
        mesh=mesh,
        in_specs=(P(None, "gx", "gy", "gz"), P("gx", "gy", "gz")),
        out_specs=(P(None, "gx", "gy", "gz"), P("gx", "gy", "gz")),
        check_vma=False,
    )
```

```python
import functools

import jax
import jax.numpy as jnp
from jax import lax
from jax.experimental import pallas as pl
from jax.experimental.pallas import tpu as pltpu
from jax.sharding import PartitionSpec as P

SWEEPS = 4
HALO = SWEEPS + 1
REACH = 3
gamma_gas = 1.4
alpha_reg = 4.0
time_step = 0.08
MESH = pl.DeviceIdType.MESH
F32 = jnp.float32
BF16 = jnp.bfloat16

SIG, EN = 4, 5
FIRST_X = 13
FIRST, MIDDLE, LAST = (0, 1), (SIG, EN), (1, SIG)
G_SIB, G_OUT, G_FAR, G_ZSAME, G_ZSIB, G_ZOUT = range(6)


def edges(c, p1, m1, p2, m2):
    even = (47.0 / 60.0) * c + (7.0 / 60.0) * (p1 + m1) - (0.5 / 60.0) * (p2 + m2)
    odd = (20.0 / 60.0) * (p1 - m1) - (2.5 / 60.0) * (p2 - m2)
    return even + odd, even - odd


def physical_flux(v, d):
    inv = 1.0 / v[0]
    u = [v[1] * inv, v[2] * inv, v[3] * inv]
    kinetic = 0.5 * (v[1] * u[0] + v[2] * u[1] + v[3] * u[2])
    p = (gamma_gas - 1.0) * (v[4] - kinetic)
    n = u[d]
    flux = [v[1 + d], v[1] * n, v[2] * n, v[3] * n, (v[4] + p) * n]
    flux[1 + d] = flux[1 + d] + p
    return flux, jnp.abs(n) + jnp.sqrt(gamma_gas * jnp.abs(p) * inv)


def face_flux(left, right, d):
    fl, sl = physical_flux(left, d)
    fr, sr = physical_flux(right, d)
    speed = jnp.maximum(sl, sr)
    return [0.5 * ((a + b) - speed * (r - l)) for a, b, l, r in zip(fl, fr, left, right)]


def up(v, axis, by=1):
    return pltpu.roll(v, (v.shape[axis] - by) % v.shape[axis], axis)


def down(v, axis, by=1):
    return pltpu.roll(v, by, axis)


def kernel(counts, cons_hbm, sigma_hbm, new_out, ent_out, cons, sigma, SGB, FP, R, ZR, STO, STS, PKS, PKO, FO, FE,
           QF, CI, U, INV, CO, SA, SB, WQ, WU, WI, WC, WS, ZB, T, send_sem, recv_sem, last_sem, in_sem):
    loads = [pltpu.make_async_copy(cons_hbm, cons, in_sem.at[0]),
             pltpu.make_async_copy(sigma_hbm, sigma, in_sem.at[1])]
    for c in loads:
        c.start()
    gx, h, gz = lax.axis_index("gx"), lax.axis_index("gy"), lax.axis_index("gz")
    nx, ny, nz = sigma.shape
    m = nx // 2
    np_ = m + 2 * HALO
    own0, sib0, end = HALO, HALO + m, HALO + 2 * m
    slot = nz // nx
    half = slot // 2
    near_rows, far_rows = slice(0, ny), slice(ny, 2 * ny)
    sg = (1 - 2 * h).astype(F32)

    right, left = lax.rem(gx + 1, counts[0]), lax.rem(gx + counts[0] - 1, counts[0])
    outer = lax.rem(gx + counts[0] - 1 + 2 * h, counts[0])
    inner = lax.rem(gx + counts[0] + 1 - 2 * h, counts[0])
    oz = 1 - gz
    rows_of = (h * 0, h * 0 + 1)

    def frame(e):
        return e + h * (np_ - 1 - 2 * e)

    def block(k):
        return k + h * (nx - 1 - 2 * k)

    lane = lax.broadcasted_iota(jnp.int32, (ny, nz), 1)
    lane2 = lax.broadcasted_iota(jnp.int32, (2 * ny, nz), 1)
    lower2 = (lane2 & (slot - 1)) < half
    first2 = lane2 < nz // 2

    def strips(parts, lanes):
        acc = None
        for at, v in parts:
            r = pltpu.roll(v, (half + slot * at) % nz, 1)
            acc = r if acc is None else jnp.where(lanes >= slot * at, r, acc)
        return acc

    def descriptors(listed, which):
        made = []
        for sec, src, dst, group, where in listed:
            made.append(pltpu.make_async_remote_copy(
                src_ref=src, dst_ref=dst, send_sem=send_sem.at[which],
                recv_sem=recv_sem.at[sec, group], device_id=where, device_id_type=MESH,
            ))
        return made

    def arrived(sec, group, ref):
        pltpu.make_async_remote_copy(
            src_ref=ref, dst_ref=ref, send_sem=send_sem.at[0], recv_sem=recv_sem.at[sec, group],
            device_id=(gx, 1 - h, gz), device_id_type=MESH,
        ).wait_recv()

    barrier = pltpu.get_barrier_semaphore()
    peers = [(gx, 1 - h, gz), (outer, h, oz), (outer, 1 - h, oz)]
    peers += [(x, y, gz) for x in (right, left) for y in (h, 1 - h)]
    peers += [(gx, h, oz), (gx, 1 - h, oz)]
    for peer in peers:
        pl.semaphore_signal(barrier, inc=1, device_id=peer, device_id_type=MESH)

    for c in loads:
        c.wait()
    SGB[...] = sigma[...].astype(BF16)
    pl.semaphore_wait(barrier, len(peers))

    def first_sends():
        listed = []

        def copy(*c):
            listed.append(c)

        for to, target, a, e, hf in ((right, 0, nx - HALO, 0, h), (left, 1, 0, sib0, 1 - h)):
            copy(0, cons.at[0:4, a:a + HALO], R.at[0, hf, 0:4, e:e + HALO], G_OUT, (to, rows_of[target], gz))
            copy(0, SGB.at[a:a + HALO], R.at[0, hf, SIG, e:e + HALO], G_OUT, (to, rows_of[target], gz))
            skip = HALO - REACH if target == 0 else 0
            copy(0, cons.at[4, a + skip:a + skip + REACH],
                 R.at[0, hf, EN, e + skip:e + skip + REACH], G_OUT, (to, rows_of[target], gz))
        for to, target, a, e, hf in ((right, 1, nx - 1, 0, 1 - h), (left, 0, 0, np_ - 1, h)):
            copy(0, cons.at[0:4, a:a + 1], R.at[0, hf, 0:4, e:e + 1], G_FAR, (to, rows_of[target], gz))
            copy(0, SGB.at[a:a + 1], R.at[0, hf, SIG, e:e + 1], G_FAR, (to, rows_of[target], gz))
        e = HALO - m + m * h
        sib = (gx, 1 - h, gz)
        copy(0, cons.at[0:4], R.at[0, 1, 0:4, pl.ds(e, nx)], G_SIB, sib)
        copy(0, SGB, R.at[0, 1, SIG, pl.ds(e, nx)], G_SIB, sib)
        copy(0, cons.at[4], R.at[0, 1, EN, pl.ds(e, nx)], G_SIB, sib)

        for target, hf in ((0, h), (1, 1 - h)):
            copy(0, FP.at[target], ZR.at[0, 0, hf], G_ZSAME, (gx, rows_of[target], oz))
            to = right if target == 0 else left
            copy(0, FP.at[target, 0:EN], ZR.at[0, 2, hf, 0:EN], G_ZOUT, (to, rows_of[target], oz))
        return descriptors(listed, 0)

    def second_sends(fields):
        listed = []

        def copy(*c):
            listed.append((1,) + c)

        back = sib0 - 2 * m * h
        over = HALO - m + 2 * m * h
        sib, across = (gx, 1 - h, gz), (outer, 1 - h, gz)
        if fields is not None:
            a, b = fields
            copy(STO.at[:, a:b], R.at[1, :, a:b, pl.ds(back, m)], G_OUT, across)
            copy(STS.at[:, a:b, 1:2], R.at[1, :, a:b, pl.ds((np_ - 1) * h, 1)], G_OUT,
                 (inner, h, gz))
            copy(STS.at[:, a:b, 0:1], R.at[1, :, a:b, pl.ds((np_ - 1) * (1 - h), 1)], G_FAR,
                 (outer, h, gz))
            if fields == LAST:
                copy(STO.at[:, EN, pl.ds(h, REACH)], R.at[1, :, EN, pl.ds(back + h, REACH)], G_OUT,
                     across)
                copy(STO.at[:, EN], R.at[1, :, EN, pl.ds(over, m)], G_SIB, sib)
            copy(STO.at[:, a:b], R.at[1, :, a:b, pl.ds(over, m)], G_SIB, sib)
        else:
            copy(PKS, ZR.at[1, 0], G_ZSAME, (gx, h, oz))
            copy(PKO, ZR.at[1, 1, :, 0:EN], G_ZSIB, (gx, 1 - h, oz))
            copy(PKO, ZR.at[1, 2, :, 0:EN], G_ZOUT, (outer, 1 - h, oz))
        return descriptors(listed, 1)

    def send_state(fields):
        for c in second_sends(fields):
            c.start()

    def advance(f):
        for k in range(m):
            rk = k + h * (m - 1 - 2 * k)
            if f == SIG:
                state = SA[own0 + k].astype(BF16)
            else:
                q = min(f, 4)
                initial = QF[q, own0 + k]
                CI[q, k] = initial
                state = (initial - time_step * T[q, k]).astype(BF16)
                QF[q, own0 + k] = state.astype(F32)
                if f == 1:
                    state = (state.astype(F32) * sg).astype(BF16)
            STO[0, f, rk], STO[1, f, rk] = state[far_rows], state[near_rows]
            if f != EN and k in (0, m - 1):
                at = 0 if k == 0 else 1
                STS[0, f, at], STS[1, f, at] = state[near_rows], state[far_rows]

    first = first_sends()
    for c in first[:FIRST_X]:
        c.start()
    for f in range(6):
        for target in (0, 1):
            parts = []
            for k in range(nx):
                p = k if target == 0 else nx - 1 - k
                parts.append((k, sigma[p] if f == SIG else cons[min(f, 4), p].astype(F32)))
            FP[target, f] = strips(parts, lane).astype(BF16)
    for c in first[FIRST_X:]:
        c.start()

    for k in range(nx):
        p = block(k)
        for f in range(5):
            v = cons.at[f][p].astype(F32)
            QF[f, own0 + k, near_rows] = v * sg if f == 1 else v
        SA[own0 + k, near_rows] = sigma[p]

    def result_copies(part):
        mh = m // 2
        a = mh * (part + h - 2 * part * h)
        return [pltpu.make_async_remote_copy(
            src_ref=src, dst_ref=dst, send_sem=last_sem.at[n], recv_sem=last_sem.at[2 + n],
            device_id=(gx, 1 - h, gz), device_id_type=MESH,
        ) for n, (src, dst) in enumerate((
            (FO.at[:, pl.ds(a, mh)], new_out.at[:, pl.ds(m * h + a, mh)]),
            (FE.at[pl.ds(a, mh)], ent_out.at[pl.ds(m * h + a, mh)])))]

    def take(sec, e, halves, fields=6):
        for hf in halves:
            rows = far_rows if hf else near_rows
            for f in range(fields):
                v = R[sec, hf, f, frame(e)].astype(F32)
                if f == SIG:
                    SA[e, rows] = v
                else:
                    QF[min(f, 4), e, rows] = v * sg if f == 1 else v

    def line_flux(fields, d, axis):
        lefts, rights = [], []
        for c in fields:
            l, r = edges(c, up(c, axis), down(c, axis), up(c, axis, 2), down(c, axis, 2))
            lefts.append(l)
            rights.append(up(r, axis))
        return [v - down(v, axis) for v in face_flux(lefts, rights, d)]

    def x_face(p):
        lefts, rights = [], []
        for f in range(5):
            v = [QF[f, p + o] for o in range(-2, 4)]
            lefts.append(edges(v[2], v[3], v[1], v[4], v[0])[0])
            rights.append(edges(v[3], v[4], v[2], v[5], v[1])[1])
        return face_flux(lefts, rights, 0)

    def velocities(p):
        inv = 1.0 / QF[0, p]
        INV[p] = inv
        for a in range(3):
            U[a, p] = QF[1 + a, p] * inv

    def stencil_terms(g, c, around):
        div = g[0][0] + g[1][1] + g[2][2]
        total = div * div + g[0][0] * g[0][0] + g[1][1] * g[1][1] + g[2][2] * g[2][2]
        total = total + 2.0 * (g[0][1] * g[1][0] + g[0][2] * g[2][0] + g[1][2] * g[2][1])
        source = (alpha_reg * 0.25) * total
        w = [(alpha_reg * 0.5) * (c + n) for n in around]
        scale = 1.0 / (c + ((w[0] + w[1]) + (w[2] + w[3]) + (w[4] + w[5])))
        return [v * scale for v in w] + [source * scale]

    def coefficients(p):
        g = []
        for a in range(3):
            u = U[a, p]
            g.append([
                U[a, p + 1] - U[a, p - 1], up(u, 0) - down(u, 0), up(u, 1) - down(u, 1),
            ])
        c = INV[p]
        around = [INV[p + 1], INV[p - 1], up(c, 0), down(c, 0), up(c, 1), down(c, 1)]
        for n, v in enumerate(stencil_terms(g, c, around)):
            CO[n, p] = v

    def jacobi(co, c, xp, xm):
        out = co(6) + co(0) * xp + co(1) * xm
        out = out + (co(2) * up(c, 0) + co(3) * down(c, 0))
        return out + (co(4) * up(c, 1) + co(5) * down(c, 1))

    def main_sweep(step, planes):
        read, write = (SA, SB) if step % 2 == 0 else (SB, SA)
        for p in planes:
            write[p] = jacobi(lambda n: CO[n, p], read[p], read[p + 1], read[p - 1])

    early = [range(own0 + 1 + t, end - 1 - t) for t in range(SWEEPS)]
    near = jnp.logical_or(lane2 < REACH, lane2 >= nz - REACH)
    edge = jnp.logical_or(lane2 < SWEEPS, lane2 >= nz - SWEEPS)
    ends = jnp.logical_or(lane2 == 0, lane2 == nz - 1)

    def ring_next(a, b):
        ua, ub = up(a, 1, slot), up(b, 1, slot)
        cut = lane2 >= nz - slot
        return jnp.where(cut, ub, ua), jnp.where(cut, ua, ub)

    def ring_prev(a, b):
        da, db = down(a, 1, slot), down(b, 1, slot)
        cut = lane2 < slot
        return jnp.where(cut, db, da), jnp.where(cut, da, db)

    def joined(own, far):
        return jnp.where(lower2, far, own), jnp.where(lower2, own, far)

    def far_strip(sec, which, f):
        v = jnp.concatenate([ZR[sec, which, hf, f].astype(F32) for hf in (0, 1)], axis=0)
        return v * sg if f == 1 else v

    def local_strip(f, planes):
        src = SA if f == SIG else QF.at[min(f, 4)]
        return strips([(at, src[p]) for at, p in planes], lane2)

    inside = [(k, own0 + k) for k in range(nx)]
    outside = [(0, end)] + [(nx - HALO + e, e) for e in range(HALO)]

    def section(sec, carry):
        arrived(sec, G_SIB, R.at[sec, :, :, 0:m])

        @pl.when(sec == 0)
        def _():
            for e in range(own0, end):
                take(0, e, (1,))

        @pl.when(sec == 1)
        def _():
            for e in range(sib0, end):
                take(1, e, (0, 1))

        for k in range(m):
            p = own0 + k
            c = [QF[f, p] for f in range(5)]
            ychange = line_flux(c, 1, 0)
            zchange = line_flux(c, 2, 1)
            for f in range(5):
                T[f, k] = ychange[f] + jnp.where(near, 0.0, zchange[f])
        h8, h7 = x_face(sib0 - 1), x_face(sib0 - 2)
        for f in range(5):
            T[f, m - 1] = T[f, m - 1] + (h8[f] - h7[f])
            T[f, m - 2] = T[f, m - 2] + h7[f]
        for p in range(own0, end):
            velocities(p)
        for p in early[0]:
            coefficients(p)
        WS[...] = local_strip(SIG, inside)
        for step in range(SWEEPS):
            main_sweep(step, early[step])

        arrived(sec, G_ZSAME, ZR.at[sec, 0])

        @pl.when(sec == 1)
        def _():
            arrived(sec, G_ZSIB, ZR.at[sec, 1, :, 0:EN])

        for f in (0, 1, 2, 3, EN):
            a = far_strip(sec, 0, f)
            if f != EN:
                a = jnp.where(first2, a, far_strip(sec, sec, f))
            WQ[min(f, 4), 0], WQ[min(f, 4), 1] = joined(local_strip(f, inside), a)
        lo = line_flux([WQ[f, 0] for f in range(5)], 2, 1)
        hi = line_flux([WQ[f, 1] for f in range(5)], 2, 1)
        for f in range(5):
            zb = jnp.where(lower2, hi[f], lo[f])
            for k in range(m):
                r = pltpu.roll(zb, nz - half - slot * k, 1)
                T[f, k] = T[f, k] + jnp.where(near, r, 0.0)

        arrived(sec, G_OUT, R.at[sec, :, 0:4, 0:7])
        arrived(sec, G_FAR, R.at[sec, :, 0:EN, 0:1])
        for e in range(HALO):
            take(sec, e, (0, 1), 6 if e >= HALO - REACH else 5)
        take(sec, end, (0, 1), 5)
        faces = [x_face(p) for p in range(own0 - 1, sib0 - 2)]
        for f in range(5):
            for k in range(m - 2):
                T[f, k] = T[f, k] + (faces[k + 1][f] - faces[k][f])
            T[f, m - 2] = T[f, m - 2] - faces[m - 2][f]

        @pl.when(sec == 0)
        def _():
            advance(0)
            send_state(FIRST)

        for p in list(range(HALO)) + [end]:
            velocities(p)
        for p in range(1, np_ - 1):
            if p not in early[0]:
                coefficients(p)

        arrived(sec, G_ZOUT, ZR.at[sec, 2, :, 0:EN])
        for f in range(4):
            WQ[f, 2], WQ[f, 3] = joined(local_strip(f, outside), far_strip(sec, 2, f))
        for n in range(4):
            inv = 1.0 / WQ[0, n]
            WI[n] = inv
            for a in range(3):
                WU[a, n] = WQ[1 + a, n] * inv
        a = jnp.where(first2, far_strip(sec, 0, SIG), far_strip(sec, sec, SIG))
        w = list(joined(WS[...], a))
        w += joined(local_strip(SIG, outside), far_strip(sec, 2, SIG))

        for b in (0, 1):
            pair = (b, 2 + b)
            g = [[], []]
            for a in range(3):
                v = [WU[a, n] for n in pair]
                nxt, prv = ring_next(*v), ring_prev(*v)
                for i in (0, 1):
                    g[i].append([nxt[i] - prv[i], up(v[i], 0) - down(v[i], 0),
                                 up(v[i], 1) - down(v[i], 1)])
            c = [WI[n] for n in pair]
            nxt, prv = ring_next(*c), ring_prev(*c)
            for i in (0, 1):
                around = [nxt[i], prv[i], up(c[i], 0), down(c[i], 0), up(c[i], 1), down(c[i], 1)]
                for n, v in enumerate(stencil_terms(g[i], c[i], around)):
                    WC[n, pair[i]] = v

        for step in range(SWEEPS):
            main_sweep(step, [p for p in range(step + 1, np_ - 1 - step) if p not in early[step]])
            fresh = [None] * 4
            for b in (0, 1):
                pair = (b, 2 + b)
                v = [w[n] for n in pair]
                nxt, prv = ring_next(*v), ring_prev(*v)
                for i in (0, 1):
                    fresh[pair[i]] = jacobi(lambda n: WC[n, pair[i]], v[i], nxt[i], prv[i])
            w = fresh
        S = SA

        for g, planes in ((0, [(k, own0 + k) for k in range(m + 1)]), (1, [(nx - 1, own0 - 1)])):
            both = jnp.where(lower2, w[2 * g + 1], w[2 * g])
            for at, p in planes:
                S[p] = jnp.where(edge, pltpu.roll(both, nz - half - slot * at, 1), S[p])

        @pl.when(sec == 0)
        def _():
            advance(SIG)
            send_state(MIDDLE)

        diffs = []
        for n in (0, 1):
            v = w[n]
            e = v * WU[2, n]
            diffs.append((up(v, 1) - down(v, 1), up(e, 1) - down(e, 1)))
        for i in (0, 1):
            ZB[i] = jnp.where(lower2, diffs[1][i], diffs[0][i])

        for k in range(m):
            p = own0 + k
            shift = nz - half - slot * k
            xp, xm = S[p + 1], S[p - 1]
            T[1, k] = T[1, k] + 0.5 * (xp - xm)
            power = xp * U[0, p + 1] - xm * U[0, p - 1]
            s = S[p]
            T[2, k] = T[2, k] + 0.5 * (up(s, 0) - down(s, 0))
            e = s * U[1, p]
            power = power + (up(e, 0) - down(e, 0))
            T[3, k] = T[3, k] + 0.5 * jnp.where(
                ends, pltpu.roll(ZB[0], shift, 1), up(s, 1) - down(s, 1))
            e = s * U[2, p]
            power = power + jnp.where(ends, pltpu.roll(ZB[1], shift, 1), up(e, 1) - down(e, 1))
            T[4, k] = T[4, k] + 0.5 * power

        @pl.when(sec == 0)
        def _():
            for f in (1, 2, 3, EN):
                advance(f)
            send_state(LAST)
            order = list(range(m)) + list(range(m - 1, -1, -1))
            for f in range(6):
                src = S if f == SIG else QF.at[min(f, 4)]
                v = strips([(at, src[own0 + k]) for at, k in enumerate(order)], lane2)
                v = (v * sg if f == 1 else v).astype(BF16)
                PKS[0, f], PKS[1, f] = v[near_rows], v[far_rows]
                if f != EN:
                    PKO[0, f], PKO[1, f] = v[far_rows], v[near_rows]
            send_state(None)

        @pl.when(sec == 1)
        def _():
            for k in range(m):
                rk = k + h * (m - 1 - 2 * k)
                for f in range(5):
                    v = 0.5 * ((CI[f, k] - time_step * T[f, k]) + QF[f, own0 + k])
                    v = v * sg if f == 1 else v
                    new_out[f, block(k)] = v[near_rows]
                    FO[f, rk] = v[far_rows]
                s = S[own0 + k]
                ent_out[block(k)] = s[near_rows]
                FE[rk] = s[far_rows]
                if k in (m // 2 - 1, m - 1):
                    for c in result_copies(2 * k // m):
                        c.start()

        return carry

    lax.fori_loop(0, 2, section, 0)

    done = list(first)
    for fields in (FIRST, MIDDLE, LAST, None):
        done += second_sends(fields)
    for c in done:
        c.wait_send()
    for part in range(2):
        for c in result_copies(part):
            c.wait_send()
    for n, ref in ((0, FO), (1, FE)):
        pltpu.make_async_remote_copy(
            src_ref=ref, dst_ref=ref, send_sem=last_sem.at[0], recv_sem=last_sem.at[2 + n],
            device_id=(gx, 1 - h, gz), device_id_type=MESH,
        ).wait_recv()


def solution(mesh):
    counts = (mesh.shape["gx"], mesh.shape["gy"], mesh.shape["gz"])
    assert counts[1] == 2 and counts[2] == 2 and counts[0] > 2

    def step(conserved, sigma_prev):
        _, nx, ny, nz = conserved.shape
        m = nx // 2
        np_ = m + 2 * HALO
        wide = (2 * ny, nz)
        slot = nz // nx
        assert nx == 2 * m and m % 2 == 0 and HALO == m + 1 and SWEEPS % 2 == 0 and nx * slot == nz
        assert slot >= 4 * SWEEPS and slot & (slot - 1) == 0
        vmem = pl.BlockSpec(memory_space=pltpu.VMEM)
        tile = (ny, nz)
        return pl.pallas_call(
            functools.partial(kernel, counts),
            out_shape=(
                pltpu.VMEM((5, nx, ny, nz), F32),
                pltpu.VMEM((nx, ny, nz), F32),
            ),
            in_specs=[pl.BlockSpec(memory_space=pltpu.HBM)] * 2,
            out_specs=(vmem, vmem),
            scratch_shapes=[
                pltpu.VMEM((5, nx) + tile, BF16),
                pltpu.VMEM((nx,) + tile, F32),
                pltpu.VMEM((nx,) + tile, BF16),
                pltpu.VMEM((2, 6) + tile, BF16),
                pltpu.VMEM((2, 2, 6, np_) + tile, BF16),
                pltpu.VMEM((2, 3, 2, 6) + tile, BF16),
                pltpu.VMEM((2, 6, m) + tile, BF16),
                pltpu.VMEM((2, 5, 2) + tile, BF16),
                pltpu.VMEM((2, 6) + tile, BF16),
                pltpu.VMEM((2, 5) + tile, BF16),
                pltpu.VMEM((5, m) + tile, F32),
                pltpu.VMEM((m,) + tile, F32),
                pltpu.VMEM((5, np_) + wide, F32),
                pltpu.VMEM((5, m) + wide, F32),
                pltpu.VMEM((3, np_) + wide, F32),
                pltpu.VMEM((np_,) + wide, F32),
                pltpu.VMEM((7, np_) + wide, F32),
                pltpu.VMEM((np_,) + wide, F32),
                pltpu.VMEM((np_,) + wide, F32),
                pltpu.VMEM((5, 4) + wide, F32),
                pltpu.VMEM((3, 4) + wide, F32),
                pltpu.VMEM((4,) + wide, F32),
                pltpu.VMEM((7, 4) + wide, F32),
                pltpu.VMEM(wide, F32),
                pltpu.VMEM((2,) + wide, F32),
                pltpu.VMEM((5, m) + wide, F32),
                pltpu.SemaphoreType.DMA((2,)),
                pltpu.SemaphoreType.DMA((2, 6)),
                pltpu.SemaphoreType.DMA((4,)),
                pltpu.SemaphoreType.DMA((2,)),
            ],
            compiler_params=pltpu.CompilerParams(collective_id=0, has_side_effects=True),
        )(conserved, sigma_prev)

    return jax.shard_map(
        step,
        mesh=mesh,
        in_specs=(P(None, "gx", "gy", "gz"), P("gx", "gy", "gz")),
        out_specs=(P(None, "gx", "gy", "gz"), P("gx", "gy", "gz")),
        check_vma=False,
    )
```

```python
import functools

import jax
import jax.numpy as jnp
from jax import lax
from jax.experimental import pallas as pl
from jax.experimental.pallas import tpu as pltpu
from jax.sharding import PartitionSpec as P

SWEEPS = 4
HALO = SWEEPS + 1
REACH = 3
gamma_gas = 1.4
alpha_reg = 4.0
time_step = 0.08
MESH = pl.DeviceIdType.MESH
F32 = jnp.float32
BF16 = jnp.bfloat16

SIG, EN = 4, 5
FIRST_X = 13
FIRST, MIDDLE, LAST = (0, 1), (SIG, EN), (1, SIG)
G_SIB, G_OUT, G_FAR, G_ZSAME, G_ZSIB, G_ZOUT = range(6)


def edges(c, p1, m1, p2, m2):
    even = (47.0 / 60.0) * c + (7.0 / 60.0) * (p1 + m1) - (0.5 / 60.0) * (p2 + m2)
    odd = (20.0 / 60.0) * (p1 - m1) - (2.5 / 60.0) * (p2 - m2)
    return even + odd, even - odd


def physical_flux(v, d):
    inv = 1.0 / v[0]
    u = [v[1] * inv, v[2] * inv, v[3] * inv]
    kinetic = 0.5 * (v[1] * u[0] + v[2] * u[1] + v[3] * u[2])
    p = (gamma_gas - 1.0) * (v[4] - kinetic)
    n = u[d]
    flux = [v[1 + d], v[1] * n, v[2] * n, v[3] * n, (v[4] + p) * n]
    flux[1 + d] = flux[1 + d] + p
    return flux, jnp.abs(n) + jnp.sqrt(gamma_gas * jnp.abs(p) * inv)


def face_flux(left, right, d):
    fl, sl = physical_flux(left, d)
    fr, sr = physical_flux(right, d)
    speed = jnp.maximum(sl, sr)
    return [0.5 * ((a + b) - speed * (r - l)) for a, b, l, r in zip(fl, fr, left, right)]


def up(v, axis, by=1):
    return pltpu.roll(v, (v.shape[axis] - by) % v.shape[axis], axis)


def down(v, axis, by=1):
    return pltpu.roll(v, by, axis)


def kernel(counts, cons_hbm, sigma_hbm, new_out, ent_out, cons, sigma, SGB, FP, FZ, R, ZR, ZO, STO, STS, PKS, PKO, PKZ,
           FO, FE,
           QF, CI, U, INV, CO, SA, SB, WQ, WU, WI, WC, WS, ZB, T, send_sem, recv_sem, last_sem, in_sem):
    loads = [pltpu.make_async_copy(cons_hbm, cons, in_sem.at[0]),
             pltpu.make_async_copy(sigma_hbm, sigma, in_sem.at[1])]
    for c in loads:
        c.start()
    gx, h, gz = lax.axis_index("gx"), lax.axis_index("gy"), lax.axis_index("gz")
    nx, ny, nz = sigma.shape
    m = nx // 2
    np_ = m + 2 * HALO
    own0, sib0, end = HALO, HALO + m, HALO + 2 * m
    slot = nz // nx
    half = slot // 2
    near_rows, far_rows = slice(0, ny), slice(ny, 2 * ny)
    sg = (1 - 2 * h).astype(F32)

    right, left = lax.rem(gx + 1, counts[0]), lax.rem(gx + counts[0] - 1, counts[0])
    outer = lax.rem(gx + counts[0] - 1 + 2 * h, counts[0])
    inner = lax.rem(gx + counts[0] + 1 - 2 * h, counts[0])
    oz = 1 - gz
    rows_of = (h * 0, h * 0 + 1)

    def frame(e):
        return e + h * (np_ - 1 - 2 * e)

    def block(k):
        return k + h * (nx - 1 - 2 * k)

    lane = lax.broadcasted_iota(jnp.int32, (ny, nz), 1)
    lane2 = lax.broadcasted_iota(jnp.int32, (2 * ny, nz), 1)
    lower2 = (lane2 & (slot - 1)) < half
    first2 = lane2 < nz // 2

    def strips(parts, lanes):
        acc = None
        for at, v in parts:
            r = pltpu.roll(v, (half + slot * at) % nz, 1)
            acc = r if acc is None else jnp.where(lanes >= slot * at, r, acc)
        return acc

    moves = (0, half, nz // 2, nz // 2 + half)

    def corner(v, lanes):
        cell = lanes & (slot - 1)
        middle = jnp.logical_and(cell >= half - SWEEPS, cell < half + SWEEPS)
        last = jnp.logical_and(lanes >= half - SWEEPS, lanes < nz // 2 + half - SWEEPS)
        r = [v[0]] + [pltpu.roll(v[j], moves[j], 1) for j in (1, 2, 3)]
        return jnp.where(middle, jnp.where(lanes >= nz // 2, r[0], r[2]),
                         jnp.where(last, r[3], r[1]))

    def descriptors(listed, which):
        made = []
        for sec, src, dst, group, where in listed:
            made.append(pltpu.make_async_remote_copy(
                src_ref=src, dst_ref=dst, send_sem=send_sem.at[which],
                recv_sem=recv_sem.at[sec, group], device_id=where, device_id_type=MESH,
            ))
        return made

    def arrived(sec, group, ref):
        pltpu.make_async_remote_copy(
            src_ref=ref, dst_ref=ref, send_sem=send_sem.at[0], recv_sem=recv_sem.at[sec, group],
            device_id=(gx, 1 - h, gz), device_id_type=MESH,
        ).wait_recv()

    barrier = pltpu.get_barrier_semaphore()
    peers = [(gx, 1 - h, gz), (outer, h, oz), (outer, 1 - h, oz)]
    peers += [(x, y, gz) for x in (right, left) for y in (h, 1 - h)]
    peers += [(gx, h, oz), (gx, 1 - h, oz)]
    for peer in peers:
        pl.semaphore_signal(barrier, inc=1, device_id=peer, device_id_type=MESH)

    for c in loads:
        c.wait()
    SGB[...] = sigma[...].astype(BF16)
    pl.semaphore_wait(barrier, len(peers))

    def first_sends():
        listed = []

        def copy(*c):
            listed.append(c)

        for to, target, a, e, hf in ((right, 0, nx - HALO, 0, h), (left, 1, 0, sib0, 1 - h)):
            copy(0, cons.at[0:4, a:a + HALO], R.at[0, hf, 0:4, e:e + HALO], G_OUT, (to, rows_of[target], gz))
            copy(0, SGB.at[a:a + HALO], R.at[0, hf, SIG, e:e + HALO], G_OUT, (to, rows_of[target], gz))
            skip = HALO - REACH if target == 0 else 0
            copy(0, cons.at[4, a + skip:a + skip + REACH],
                 R.at[0, hf, EN, e + skip:e + skip + REACH], G_OUT, (to, rows_of[target], gz))
        for to, target, a, e, hf in ((right, 1, nx - 1, 0, 1 - h), (left, 0, 0, np_ - 1, h)):
            copy(0, cons.at[0:4, a:a + 1], R.at[0, hf, 0:4, e:e + 1], G_FAR, (to, rows_of[target], gz))
            copy(0, SGB.at[a:a + 1], R.at[0, hf, SIG, e:e + 1], G_FAR, (to, rows_of[target], gz))
        e = HALO - m + m * h
        sib = (gx, 1 - h, gz)
        copy(0, cons.at[0:4], R.at[0, 1, 0:4, pl.ds(e, nx)], G_SIB, sib)
        copy(0, SGB, R.at[0, 1, SIG, pl.ds(e, nx)], G_SIB, sib)
        copy(0, cons.at[4], R.at[0, 1, EN, pl.ds(e, nx)], G_SIB, sib)

        for target, hf in ((0, h), (1, 1 - h)):
            copy(0, FP.at[target], ZR.at[0, 0, hf], G_ZSAME, (gx, rows_of[target], oz))
            to = right if target == 0 else left
            copy(0, FZ.at[target], ZO.at[0, hf], G_ZOUT, (to, rows_of[target], oz))
        return descriptors(listed, 0)

    def second_sends(fields):
        listed = []

        def copy(*c):
            listed.append((1,) + c)

        back = sib0 - 2 * m * h
        over = HALO - m + 2 * m * h
        sib, across = (gx, 1 - h, gz), (outer, 1 - h, gz)
        if fields is not None:
            a, b = fields
            copy(STO.at[:, a:b], R.at[1, :, a:b, pl.ds(back, m)], G_OUT, across)
            copy(STS.at[:, a:b, 1:2], R.at[1, :, a:b, pl.ds((np_ - 1) * h, 1)], G_OUT,
                 (inner, h, gz))
            copy(STS.at[:, a:b, 0:1], R.at[1, :, a:b, pl.ds((np_ - 1) * (1 - h), 1)], G_FAR,
                 (outer, h, gz))
            if fields == LAST:
                copy(STO.at[:, EN, pl.ds(h, REACH)], R.at[1, :, EN, pl.ds(back + h, REACH)], G_OUT,
                     across)
                copy(STO.at[:, EN], R.at[1, :, EN, pl.ds(over, m)], G_SIB, sib)
            copy(STO.at[:, a:b], R.at[1, :, a:b, pl.ds(over, m)], G_SIB, sib)
        else:
            copy(PKS, ZR.at[1, 0], G_ZSAME, (gx, h, oz))
            copy(PKO, ZR.at[1, 1, :, 0:EN], G_ZSIB, (gx, 1 - h, oz))
            copy(PKZ.at[0:2], ZO.at[1, :, 0], G_ZOUT, (outer, 1 - h, oz))
            copy(PKZ.at[2], ZO.at[1, 0, 1], G_ZOUT, (outer, 1 - h, oz))
        return descriptors(listed, 1)

    def send_state(fields):
        for c in second_sends(fields):
            c.start()

    def advance(f):
        for k in range(m):
            rk = k + h * (m - 1 - 2 * k)
            if f == SIG:
                state = SA[own0 + k].astype(BF16)
            else:
                q = min(f, 4)
                initial = QF[q, own0 + k]
                CI[q, k] = initial
                state = (initial - time_step * T[q, k]).astype(BF16)
                QF[q, own0 + k] = state.astype(F32)
                if f == 1:
                    state = (state.astype(F32) * sg).astype(BF16)
            STO[0, f, rk], STO[1, f, rk] = state[far_rows], state[near_rows]
            if f != EN and k in (0, m - 1):
                at = 0 if k == 0 else 1
                STS[0, f, at], STS[1, f, at] = state[near_rows], state[far_rows]

    first = first_sends()
    for c in first[:FIRST_X]:
        c.start()
    packed = [[], []]
    for f in range(6):
        for target in (0, 1):
            parts = []
            for k in range(nx):
                p = k if target == 0 else nx - 1 - k
                parts.append((k, sigma[p] if f == SIG else cons[min(f, 4), p].astype(F32)))
            v = strips(parts, lane)
            FP[target, f] = v.astype(BF16)
            packed[target].append(v)
    for target in (0, 1):
        FZ[target, 0] = corner(packed[target], lane).astype(BF16)
        FZ[target, 1] = packed[target][SIG].astype(BF16)
    for c in first[FIRST_X:]:
        c.start()

    for k in range(nx):
        p = block(k)
        for f in range(5):
            v = cons.at[f][p].astype(F32)
            QF[f, own0 + k, near_rows] = v * sg if f == 1 else v
        SA[own0 + k, near_rows] = sigma[p]

    def result_copies(part):
        mh = m // 2
        a = mh * (part + h - 2 * part * h)
        return [pltpu.make_async_remote_copy(
            src_ref=src, dst_ref=dst, send_sem=last_sem.at[n], recv_sem=last_sem.at[2 + n],
            device_id=(gx, 1 - h, gz), device_id_type=MESH,
        ) for n, (src, dst) in enumerate((
            (FO.at[:, pl.ds(a, mh)], new_out.at[:, pl.ds(m * h + a, mh)]),
            (FE.at[pl.ds(a, mh)], ent_out.at[pl.ds(m * h + a, mh)])))]

    def take(sec, e, halves, fields=6):
        for hf in halves:
            rows = far_rows if hf else near_rows
            for f in range(fields):
                v = R[sec, hf, f, frame(e)].astype(F32)
                if f == SIG:
                    SA[e, rows] = v
                else:
                    QF[min(f, 4), e, rows] = v * sg if f == 1 else v

    def line_flux(fields, d, axis):
        lefts, rights = [], []
        for c in fields:
            l, r = edges(c, up(c, axis), down(c, axis), up(c, axis, 2), down(c, axis, 2))
            lefts.append(l)
            rights.append(up(r, axis))
        return [v - down(v, axis) for v in face_flux(lefts, rights, d)]

    def x_face(p):
        lefts, rights = [], []
        for f in range(5):
            v = [QF[f, p + o] for o in range(-2, 4)]
            lefts.append(edges(v[2], v[3], v[1], v[4], v[0])[0])
            rights.append(edges(v[3], v[4], v[2], v[5], v[1])[1])
        return face_flux(lefts, rights, 0)

    def velocities(p):
        inv = 1.0 / QF[0, p]
        INV[p] = inv
        for a in range(3):
            U[a, p] = QF[1 + a, p] * inv

    def stencil_terms(g, c, around):
        div = g[0][0] + g[1][1] + g[2][2]
        total = div * div + g[0][0] * g[0][0] + g[1][1] * g[1][1] + g[2][2] * g[2][2]
        total = total + 2.0 * (g[0][1] * g[1][0] + g[0][2] * g[2][0] + g[1][2] * g[2][1])
        source = (alpha_reg * 0.25) * total
        w = [(alpha_reg * 0.5) * (c + n) for n in around]
        scale = 1.0 / (c + ((w[0] + w[1]) + (w[2] + w[3]) + (w[4] + w[5])))
        return [v * scale for v in w] + [source * scale]

    def coefficients(p):
        g = []
        for a in range(3):
            u = U[a, p]
            g.append([
                U[a, p + 1] - U[a, p - 1], up(u, 0) - down(u, 0), up(u, 1) - down(u, 1),
            ])
        c = INV[p]
        around = [INV[p + 1], INV[p - 1], up(c, 0), down(c, 0), up(c, 1), down(c, 1)]
        for n, v in enumerate(stencil_terms(g, c, around)):
            CO[n, p] = v

    def jacobi(co, c, xp, xm):
        out = co(6) + co(0) * xp + co(1) * xm
        out = out + (co(2) * up(c, 0) + co(3) * down(c, 0))
        return out + (co(4) * up(c, 1) + co(5) * down(c, 1))

    def main_sweep(step, planes):
        read, write = (SA, SB) if step % 2 == 0 else (SB, SA)
        for p in planes:
            write[p] = jacobi(lambda n: CO[n, p], read[p], read[p + 1], read[p - 1])

    early = [range(own0 + 1 + t, end - 1 - t) for t in range(SWEEPS)]
    near = jnp.logical_or(lane2 < REACH, lane2 >= nz - REACH)
    edge = jnp.logical_or(lane2 < SWEEPS, lane2 >= nz - SWEEPS)
    ends = jnp.logical_or(lane2 == 0, lane2 == nz - 1)

    def ring_next(a, b):
        ua, ub = up(a, 1, slot), up(b, 1, slot)
        cut = lane2 >= nz - slot
        return jnp.where(cut, ub, ua), jnp.where(cut, ua, ub)

    def ring_prev(a, b):
        da, db = down(a, 1, slot), down(b, 1, slot)
        cut = lane2 < slot
        return jnp.where(cut, db, da), jnp.where(cut, da, db)

    def joined(own, far):
        return jnp.where(lower2, far, own), jnp.where(lower2, own, far)

    def far_strip(sec, which, f):
        v = jnp.concatenate([ZR[sec, which, hf, f].astype(F32) for hf in (0, 1)], axis=0)
        return v * sg if f == 1 else v

    def outer_strips(sec):
        v = jnp.concatenate([ZO[sec, hf, 0].astype(F32) for hf in (0, 1)], axis=0)
        fields = [v] + [pltpu.roll(v, nz - moves[j], 1) for j in (1, 2, 3)]
        fields[1] = fields[1] * sg
        a, b = ZO[sec, 0, 1].astype(F32), ZO[sec, 1, 1].astype(F32)
        b = jnp.where(sec == 0, b, pltpu.roll(a, nz // 2, 1))
        return fields + [jnp.concatenate([a, b], axis=0)]

    def local_strip(f, planes):
        src = SA if f == SIG else QF.at[min(f, 4)]
        return strips([(at, src[p]) for at, p in planes], lane2)

    inside = [(k, own0 + k) for k in range(nx)]
    outside = [(0, end)] + [(nx - HALO + e, e) for e in range(HALO)]

    def section(sec, carry):
        arrived(sec, G_SIB, R.at[sec, :, :, 0:m])

        @pl.when(sec == 0)
        def _():
            for e in range(own0, end):
                take(0, e, (1,))

        @pl.when(sec == 1)
        def _():
            for e in range(sib0, end):
                take(1, e, (0, 1))

        for k in range(m):
            p = own0 + k
            c = [QF[f, p] for f in range(5)]
            ychange = line_flux(c, 1, 0)
            zchange = line_flux(c, 2, 1)
            for f in range(5):
                T[f, k] = ychange[f] + jnp.where(near, 0.0, zchange[f])
        h8, h7 = x_face(sib0 - 1), x_face(sib0 - 2)
        for f in range(5):
            T[f, m - 1] = T[f, m - 1] + (h8[f] - h7[f])
            T[f, m - 2] = T[f, m - 2] + h7[f]
        for p in range(own0, end):
            velocities(p)
        for p in early[0]:
            coefficients(p)
        WS[...] = local_strip(SIG, inside)
        for step in range(SWEEPS):
            main_sweep(step, early[step])

        arrived(sec, G_ZSAME, ZR.at[sec, 0])

        @pl.when(sec == 1)
        def _():
            arrived(sec, G_ZSIB, ZR.at[sec, 1, :, 0:EN])

        for f in (0, 1, 2, 3, EN):
            a = far_strip(sec, 0, f)
            if f != EN:
                a = jnp.where(first2, a, far_strip(sec, sec, f))
            WQ[min(f, 4), 0], WQ[min(f, 4), 1] = joined(local_strip(f, inside), a)
        lo = line_flux([WQ[f, 0] for f in range(5)], 2, 1)
        hi = line_flux([WQ[f, 1] for f in range(5)], 2, 1)
        for f in range(5):
            zb = jnp.where(lower2, hi[f], lo[f])
            for k in range(m):
                r = pltpu.roll(zb, nz - half - slot * k, 1)
                T[f, k] = T[f, k] + jnp.where(near, r, 0.0)

        arrived(sec, G_OUT, R.at[sec, :, 0:4, 0:7])
        arrived(sec, G_FAR, R.at[sec, :, 0:EN, 0:1])
        for e in range(HALO):
            take(sec, e, (0, 1), 6 if e >= HALO - REACH else 5)
        take(sec, end, (0, 1), 5)
        faces = [x_face(p) for p in range(own0 - 1, sib0 - 2)]
        for f in range(5):
            for k in range(m - 2):
                T[f, k] = T[f, k] + (faces[k + 1][f] - faces[k][f])
            T[f, m - 2] = T[f, m - 2] - faces[m - 2][f]

        @pl.when(sec == 0)
        def _():
            advance(0)
            send_state(FIRST)

        for p in list(range(HALO)) + [end]:
            velocities(p)
        for p in range(1, np_ - 1):
            if p not in early[0]:
                coefficients(p)

        @pl.when(sec == 0)
        def _():
            arrived(0, G_ZOUT, ZO.at[0])

        @pl.when(sec == 1)
        def _():
            arrived(1, G_ZOUT, R.at[1, 0, 0, 0:3])

        outer_far = outer_strips(sec)
        for f in range(4):
            WQ[f, 2], WQ[f, 3] = joined(local_strip(f, outside), outer_far[f])
        for n in range(4):
            inv = 1.0 / WQ[0, n]
            WI[n] = inv
            for a in range(3):
                WU[a, n] = WQ[1 + a, n] * inv
        a = jnp.where(first2, far_strip(sec, 0, SIG), far_strip(sec, sec, SIG))
        w = list(joined(WS[...], a))
        w += joined(local_strip(SIG, outside), outer_far[SIG])

        for b in (0, 1):
            pair = (b, 2 + b)
            g = [[], []]
            for a in range(3):
                v = [WU[a, n] for n in pair]
                nxt, prv = ring_next(*v), ring_prev(*v)
                for i in (0, 1):
                    g[i].append([nxt[i] - prv[i], up(v[i], 0) - down(v[i], 0),
                                 up(v[i], 1) - down(v[i], 1)])
            c = [WI[n] for n in pair]
            nxt, prv = ring_next(*c), ring_prev(*c)
            for i in (0, 1):
                around = [nxt[i], prv[i], up(c[i], 0), down(c[i], 0), up(c[i], 1), down(c[i], 1)]
                for n, v in enumerate(stencil_terms(g[i], c[i], around)):
                    WC[n, pair[i]] = v

        for step in range(SWEEPS):
            main_sweep(step, [p for p in range(step + 1, np_ - 1 - step) if p not in early[step]])
            fresh = [None] * 4
            for b in (0, 1):
                pair = (b, 2 + b)
                v = [w[n] for n in pair]
                nxt, prv = ring_next(*v), ring_prev(*v)
                for i in (0, 1):
                    fresh[pair[i]] = jacobi(lambda n: WC[n, pair[i]], v[i], nxt[i], prv[i])
            w = fresh
        S = SA

        for g, planes in ((0, [(k, own0 + k) for k in range(m + 1)]), (1, [(nx - 1, own0 - 1)])):
            both = jnp.where(lower2, w[2 * g + 1], w[2 * g])
            for at, p in planes:
                S[p] = jnp.where(edge, pltpu.roll(both, nz - half - slot * at, 1), S[p])

        @pl.when(sec == 0)
        def _():
            advance(SIG)
            send_state(MIDDLE)

        diffs = []
        for n in (0, 1):
            v = w[n]
            e = v * WU[2, n]
            diffs.append((up(v, 1) - down(v, 1), up(e, 1) - down(e, 1)))
        for i in (0, 1):
            ZB[i] = jnp.where(lower2, diffs[1][i], diffs[0][i])

        for k in range(m):
            p = own0 + k
            shift = nz - half - slot * k
            xp, xm = S[p + 1], S[p - 1]
            T[1, k] = T[1, k] + 0.5 * (xp - xm)
            power = xp * U[0, p + 1] - xm * U[0, p - 1]
            s = S[p]
            T[2, k] = T[2, k] + 0.5 * (up(s, 0) - down(s, 0))
            e = s * U[1, p]
            power = power + (up(e, 0) - down(e, 0))
            T[3, k] = T[3, k] + 0.5 * jnp.where(
                ends, pltpu.roll(ZB[0], shift, 1), up(s, 1) - down(s, 1))
            e = s * U[2, p]
            power = power + jnp.where(ends, pltpu.roll(ZB[1], shift, 1), up(e, 1) - down(e, 1))
            T[4, k] = T[4, k] + 0.5 * power

        @pl.when(sec == 0)
        def _():
            for f in (1, 2, 3, EN):
                advance(f)
            send_state(LAST)
            order = list(range(m)) + list(range(m - 1, -1, -1))
            packs = []
            for f in range(6):
                src = S if f == SIG else QF.at[min(f, 4)]
                v = strips([(at, src[own0 + k]) for at, k in enumerate(order)], lane2)
                v = v * sg if f == 1 else v
                packs.append(v)
                v = v.astype(BF16)
                PKS[0, f], PKS[1, f] = v[near_rows], v[far_rows]
                if f != EN:
                    PKO[0, f], PKO[1, f] = v[far_rows], v[near_rows]
            v = corner(packs, lane2).astype(BF16)
            PKZ[0], PKZ[1] = v[far_rows], v[near_rows]
            v = packs[SIG]
            PKZ[2] = jnp.where(lane >= nz // 2, v[far_rows],
                               pltpu.roll(v[near_rows], nz // 2, 1)).astype(BF16)
            send_state(None)

        @pl.when(sec == 1)
        def _():
            for k in range(m):
                rk = k + h * (m - 1 - 2 * k)
                for f in range(5):
                    v = 0.5 * ((CI[f, k] - time_step * T[f, k]) + QF[f, own0 + k])
                    v = v * sg if f == 1 else v
                    new_out[f, block(k)] = v[near_rows]
                    FO[f, rk] = v[far_rows]
                s = S[own0 + k]
                ent_out[block(k)] = s[near_rows]
                FE[rk] = s[far_rows]
                if k in (m // 2 - 1, m - 1):
                    for c in result_copies(2 * k // m):
                        c.start()

        return carry

    lax.fori_loop(0, 2, section, 0)

    done = list(first)
    for fields in (FIRST, MIDDLE, LAST, None):
        done += second_sends(fields)
    for c in done:
        c.wait_send()
    for part in range(2):
        for c in result_copies(part):
            c.wait_send()
    for n, ref in ((0, FO), (1, FE)):
        pltpu.make_async_remote_copy(
            src_ref=ref, dst_ref=ref, send_sem=last_sem.at[0], recv_sem=last_sem.at[2 + n],
            device_id=(gx, 1 - h, gz), device_id_type=MESH,
        ).wait_recv()


def solution(mesh):
    counts = (mesh.shape["gx"], mesh.shape["gy"], mesh.shape["gz"])
    assert counts[1] == 2 and counts[2] == 2 and counts[0] > 2

    def step(conserved, sigma_prev):
        _, nx, ny, nz = conserved.shape
        m = nx // 2
        np_ = m + 2 * HALO
        wide = (2 * ny, nz)
        slot = nz // nx
        assert nx == 2 * m and m % 2 == 0 and HALO == m + 1 and SWEEPS % 2 == 0 and nx * slot == nz
        assert slot >= 4 * SWEEPS and slot & (slot - 1) == 0
        vmem = pl.BlockSpec(memory_space=pltpu.VMEM)
        tile = (ny, nz)
        return pl.pallas_call(
            functools.partial(kernel, counts),
            out_shape=(
                pltpu.VMEM((5, nx, ny, nz), F32),
                pltpu.VMEM((nx, ny, nz), F32),
            ),
            in_specs=[pl.BlockSpec(memory_space=pltpu.HBM)] * 2,
            out_specs=(vmem, vmem),
            scratch_shapes=[
                pltpu.VMEM((5, nx) + tile, BF16),
                pltpu.VMEM((nx,) + tile, F32),
                pltpu.VMEM((nx,) + tile, BF16),
                pltpu.VMEM((2, 6) + tile, BF16),
                pltpu.VMEM((2, 2) + tile, BF16),
                pltpu.VMEM((2, 2, 6, np_) + tile, BF16),
                pltpu.VMEM((2, 2, 2, 6) + tile, BF16),
                pltpu.VMEM((2, 2, 2) + tile, BF16),
                pltpu.VMEM((2, 6, m) + tile, BF16),
                pltpu.VMEM((2, 5, 2) + tile, BF16),
                pltpu.VMEM((2, 6) + tile, BF16),
                pltpu.VMEM((2, 5) + tile, BF16),
                pltpu.VMEM((3,) + tile, BF16),
                pltpu.VMEM((5, m) + tile, F32),
                pltpu.VMEM((m,) + tile, F32),
                pltpu.VMEM((5, np_) + wide, F32),
                pltpu.VMEM((5, m) + wide, F32),
                pltpu.VMEM((3, np_) + wide, F32),
                pltpu.VMEM((np_,) + wide, F32),
                pltpu.VMEM((7, np_) + wide, F32),
                pltpu.VMEM((np_,) + wide, F32),
                pltpu.VMEM((np_,) + wide, F32),
                pltpu.VMEM((5, 4) + wide, F32),
                pltpu.VMEM((3, 4) + wide, F32),
                pltpu.VMEM((4,) + wide, F32),
                pltpu.VMEM((7, 4) + wide, F32),
                pltpu.VMEM(wide, F32),
                pltpu.VMEM((2,) + wide, F32),
                pltpu.VMEM((5, m) + wide, F32),
                pltpu.SemaphoreType.DMA((2,)),
                pltpu.SemaphoreType.DMA((2, 6)),
                pltpu.SemaphoreType.DMA((4,)),
                pltpu.SemaphoreType.DMA((2,)),
            ],
            compiler_params=pltpu.CompilerParams(collective_id=0, has_side_effects=True),
        )(conserved, sigma_prev)

    return jax.shard_map(
        step,
        mesh=mesh,
        in_specs=(P(None, "gx", "gy", "gz"), P("gx", "gy", "gz")),
        out_specs=(P(None, "gx", "gy", "gz"), P("gx", "gy", "gz")),
        check_vma=False,
    )
```

```python
import functools

import jax
import jax.numpy as jnp
from jax import lax
from jax.experimental import pallas as pl
from jax.experimental.pallas import tpu as pltpu
from jax.sharding import PartitionSpec as P

SWEEPS = 4
HALO = SWEEPS + 1
REACH = 3
gamma_gas = 1.4
alpha_reg = 4.0
time_step = 0.08
MESH = pl.DeviceIdType.MESH
F32 = jnp.float32
BF16 = jnp.bfloat16

SIG, EN = 4, 5
FIRST, MIDDLE, LAST = (0, 1), (SIG, EN), (1, SIG)
G_SIB, G_OUT, G_FAR, G_ZSAME, G_ZSIB, G_ZOUT, G_EN = range(7)


def edges(c, p1, m1, p2, m2):
    even = (47.0 / 60.0) * c + (7.0 / 60.0) * (p1 + m1) - (0.5 / 60.0) * (p2 + m2)
    odd = (20.0 / 60.0) * (p1 - m1) - (2.5 / 60.0) * (p2 - m2)
    return even + odd, even - odd


def physical_flux(v, d):
    inv = 1.0 / v[0]
    u = [v[1] * inv, v[2] * inv, v[3] * inv]
    kinetic = 0.5 * (v[1] * u[0] + v[2] * u[1] + v[3] * u[2])
    p = (gamma_gas - 1.0) * (v[4] - kinetic)
    n = u[d]
    flux = [v[1 + d], v[1] * n, v[2] * n, v[3] * n, (v[4] + p) * n]
    flux[1 + d] = flux[1 + d] + p
    return flux, jnp.abs(n) + jnp.sqrt(gamma_gas * jnp.abs(p) * inv)


def face_flux(left, right, d):
    fl, sl = physical_flux(left, d)
    fr, sr = physical_flux(right, d)
    speed = jnp.maximum(sl, sr)
    return [0.5 * ((a + b) - speed * (r - l)) for a, b, l, r in zip(fl, fr, left, right)]


def up(v, axis, by=1):
    return pltpu.roll(v, (v.shape[axis] - by) % v.shape[axis], axis)


def down(v, axis, by=1):
    return pltpu.roll(v, by, axis)


def kernel(counts, cons_hbm, sigma_hbm, new_out, ent_out, cons, sigma, SGB, FP, FZ, R, ZR, ZO, STO, STS, PKS, PKO, PKZ,
           FO, FE,
           QF, CI, U, INV, CO, SA, SB, WQ, WU, WI, WC, WS, ZB, T, send_sem, recv_sem, last_sem, in_sem):
    loads = [pltpu.make_async_copy(cons_hbm, cons, in_sem.at[0]),
             pltpu.make_async_copy(sigma_hbm, sigma, in_sem.at[1])]
    for c in loads:
        c.start()
    gx, h, gz = lax.axis_index("gx"), lax.axis_index("gy"), lax.axis_index("gz")
    nx, ny, nz = sigma.shape
    m = nx // 2
    np_ = m + 2 * HALO
    own0, sib0, end = HALO, HALO + m, HALO + 2 * m
    slot = nz // nx
    half = slot // 2
    near_rows, far_rows = slice(0, ny), slice(ny, 2 * ny)
    sg = (1 - 2 * h).astype(F32)

    right, left = lax.rem(gx + 1, counts[0]), lax.rem(gx + counts[0] - 1, counts[0])
    outer = lax.rem(gx + counts[0] - 1 + 2 * h, counts[0])
    inner = lax.rem(gx + counts[0] + 1 - 2 * h, counts[0])
    oz = 1 - gz
    rows_of = (h * 0, h * 0 + 1)

    def frame(e):
        return e + h * (np_ - 1 - 2 * e)

    def block(k):
        return k + h * (nx - 1 - 2 * k)

    lane = lax.broadcasted_iota(jnp.int32, (ny, nz), 1)
    lane2 = lax.broadcasted_iota(jnp.int32, (2 * ny, nz), 1)
    lower2 = (lane2 & (slot - 1)) < half
    first2 = lane2 < nz // 2

    def strips(parts, lanes):
        acc = None
        for at, v in parts:
            r = pltpu.roll(v, (half + slot * at) % nz, 1)
            acc = r if acc is None else jnp.where(lanes >= slot * at, r, acc)
        return acc

    def descriptors(listed, which):
        made = []
        for sec, src, dst, group, where in listed:
            made.append(pltpu.make_async_remote_copy(
                src_ref=src, dst_ref=dst, send_sem=send_sem.at[which],
                recv_sem=recv_sem.at[sec, group], device_id=where, device_id_type=MESH,
            ))
        return made

    def arrived(sec, group, ref):
        pltpu.make_async_remote_copy(
            src_ref=ref, dst_ref=ref, send_sem=send_sem.at[0], recv_sem=recv_sem.at[sec, group],
            device_id=(gx, 1 - h, gz), device_id_type=MESH,
        ).wait_recv()

    barrier = pltpu.get_barrier_semaphore()
    peers = [(gx, 1 - h, gz), (outer, h, oz), (outer, 1 - h, oz)]
    peers += [(x, y, gz) for x in (right, left) for y in (h, 1 - h)]
    peers += [(gx, h, oz), (gx, 1 - h, oz)]
    for peer in peers:
        pl.semaphore_signal(barrier, inc=1, device_id=peer, device_id_type=MESH)

    for c in loads:
        c.wait()
    SGB[...] = sigma[...].astype(BF16)
    moves = (0, half, nz // 2, nz // 2 + half)

    def corner(v, lanes):
        cell = lanes & (slot - 1)
        middle = jnp.logical_and(cell >= half - SWEEPS, cell < half + SWEEPS)
        last = jnp.logical_and(lanes >= half - SWEEPS, lanes < nz // 2 + half - SWEEPS)
        r = [v[0]] + [pltpu.roll(v[j], moves[j], 1) for j in (1, 2, 3)]
        return jnp.where(middle, jnp.where(lanes >= nz // 2, r[0], r[2]),
                         jnp.where(last, r[3], r[1]))

    packed = [[], []]
    for f in range(6):
        for target in (0, 1):
            parts = []
            for k in range(nx):
                p = k if target == 0 else nx - 1 - k
                parts.append((k, sigma[p] if f == SIG else cons[min(f, 4), p].astype(F32)))
            v = strips(parts, lane)
            FP[target, f] = v.astype(BF16)
            packed[target].append(v)
    for target in (0, 1):
        FZ[target, 0] = corner(packed[target], lane).astype(BF16)
        FZ[target, 1] = packed[target][SIG].astype(BF16)
    pl.semaphore_wait(barrier, len(peers))

    def first_sends():
        listed = []

        def copy(*c):
            listed.append(c)

        odd = lax.rem(gx, 2)
        sides = []
        for side in (odd, 1 - odd):
            to = left + side * (right - left)
            hf = h * side + (1 - h) * (1 - side)
            sides.append((side, hf, (to, 1 - side, gz), (to, side, gz)))
        for side, hf, to, _ in sides:
            a, e = (nx - HALO) * side, sib0 * (1 - side)
            skip = (HALO - REACH) * side
            copy(0, cons.at[0:4, pl.ds(a, HALO)], R.at[0, hf, 0:4, pl.ds(e, HALO)], G_OUT, to)
            copy(0, cons.at[4, pl.ds(a + skip, REACH)], R.at[0, hf, EN, pl.ds(e + skip, REACH)],
                 G_EN, to)
        for target, hf in ((0, h), (1, 1 - h)):
            to = right if target == 0 else left
            copy(0, FZ.at[target], ZO.at[0, hf], G_ZOUT, (to, rows_of[target], oz))
        for side, hf, to, over in sides:
            a, e = (nx - HALO) * side, sib0 * (1 - side)
            copy(0, SGB.at[pl.ds(a, HALO)], R.at[0, hf, SIG, pl.ds(e, HALO)], G_FAR, to)
            a, e = (nx - 1) * side, (np_ - 1) * (1 - side)
            copy(0, cons.at[0:4, pl.ds(a, 1)], R.at[0, 1 - hf, 0:4, pl.ds(e, 1)], G_FAR, over)
            copy(0, SGB.at[pl.ds(a, 1)], R.at[0, 1 - hf, SIG, pl.ds(e, 1)], G_FAR, over)
        e = HALO - m + m * h
        sib = (gx, 1 - h, gz)
        copy(0, cons.at[0:4], R.at[0, 1, 0:4, pl.ds(e, nx)], G_SIB, sib)
        copy(0, SGB, R.at[0, 1, SIG, pl.ds(e, nx)], G_SIB, sib)
        copy(0, cons.at[4], R.at[0, 1, EN, pl.ds(e, nx)], G_SIB, sib)

        for target, hf in ((0, h), (1, 1 - h)):
            copy(0, FP.at[target], ZR.at[0, 0, hf], G_ZSAME, (gx, rows_of[target], oz))
        return descriptors(listed, 0)

    def second_sends(fields):
        listed = []

        def copy(*c):
            listed.append((1,) + c)

        back = sib0 - 2 * m * h
        over = HALO - m + 2 * m * h
        sib, across = (gx, 1 - h, gz), (outer, 1 - h, gz)
        if fields is not None:
            a, b = fields
            group = G_FAR if fields == MIDDLE else G_OUT
            copy(STO.at[:, a:b], R.at[1, :, a:b, pl.ds(back, m)], group, across)
            copy(STS.at[:, a:b, 1:2], R.at[1, :, a:b, pl.ds((np_ - 1) * h, 1)], group,
                 (inner, h, gz))
            copy(STS.at[:, a:b, 0:1], R.at[1, :, a:b, pl.ds((np_ - 1) * (1 - h), 1)], G_FAR,
                 (outer, h, gz))
            if fields == LAST:
                copy(STO.at[:, EN, pl.ds(h, REACH)], R.at[1, :, EN, pl.ds(back + h, REACH)], G_EN,
                     across)
                copy(STO.at[:, EN], R.at[1, :, EN, pl.ds(over, m)], G_SIB, sib)
            copy(STO.at[:, a:b], R.at[1, :, a:b, pl.ds(over, m)], G_SIB, sib)
        else:
            copy(PKS, ZR.at[1, 0], G_ZSAME, (gx, h, oz))
            copy(PKO, ZR.at[1, 1, :, 0:EN], G_ZSIB, (gx, 1 - h, oz))
            copy(PKZ.at[0:2], ZO.at[1, :, 0], G_ZOUT, (outer, 1 - h, oz))
            copy(PKZ.at[2], ZO.at[1, 0, 1], G_ZOUT, (outer, 1 - h, oz))
        return descriptors(listed, 1)

    def send_state(fields):
        for c in second_sends(fields):
            c.start()

    def advance(f):
        for k in range(m):
            rk = k + h * (m - 1 - 2 * k)
            if f == SIG:
                state = SA[own0 + k].astype(BF16)
            else:
                q = min(f, 4)
                initial = QF[q, own0 + k]
                CI[q, k] = initial
                state = (initial - time_step * T[q, k]).astype(BF16)
                QF[q, own0 + k] = state.astype(F32)
                if f == 1:
                    state = (state.astype(F32) * sg).astype(BF16)
            STO[0, f, rk], STO[1, f, rk] = state[far_rows], state[near_rows]
            if f != EN and k in (0, m - 1):
                at = 0 if k == 0 else 1
                STS[0, f, at], STS[1, f, at] = state[near_rows], state[far_rows]

    first = first_sends()
    for c in first:
        c.start()

    for k in range(nx):
        p = block(k)
        for f in range(5):
            v = cons.at[f][p].astype(F32)
            QF[f, own0 + k, near_rows] = v * sg if f == 1 else v
        SA[own0 + k, near_rows] = sigma[p]

    def result_copies(part):
        mh = m // 2
        a = mh * (part + h - 2 * part * h)
        return [pltpu.make_async_remote_copy(
            src_ref=src, dst_ref=dst, send_sem=last_sem.at[n], recv_sem=last_sem.at[2 + n],
            device_id=(gx, 1 - h, gz), device_id_type=MESH,
        ) for n, (src, dst) in enumerate((
            (FO.at[:, pl.ds(a, mh)], new_out.at[:, pl.ds(m * h + a, mh)]),
            (FE.at[pl.ds(a, mh)], ent_out.at[pl.ds(m * h + a, mh)])))]

    def take(sec, e, halves, fields=range(6)):
        for hf in halves:
            rows = far_rows if hf else near_rows
            for f in fields:
                v = R[sec, hf, f, frame(e)].astype(F32)
                if f == SIG:
                    SA[e, rows] = v
                else:
                    QF[min(f, 4), e, rows] = v * sg if f == 1 else v

    def line_flux(fields, d, axis):
        lefts, rights = [], []
        for c in fields:
            l, r = edges(c, up(c, axis), down(c, axis), up(c, axis, 2), down(c, axis, 2))
            lefts.append(l)
            rights.append(up(r, axis))
        return [v - down(v, axis) for v in face_flux(lefts, rights, d)]

    def x_face(p):
        lefts, rights = [], []
        for f in range(5):
            v = [QF[f, p + o] for o in range(-2, 4)]
            lefts.append(edges(v[2], v[3], v[1], v[4], v[0])[0])
            rights.append(edges(v[3], v[4], v[2], v[5], v[1])[1])
        return face_flux(lefts, rights, 0)

    def velocities(p):
        inv = 1.0 / QF[0, p]
        INV[p] = inv
        for a in range(3):
            U[a, p] = QF[1 + a, p] * inv

    def stencil_terms(g, c, around):
        div = g[0][0] + g[1][1] + g[2][2]
        total = div * div + g[0][0] * g[0][0] + g[1][1] * g[1][1] + g[2][2] * g[2][2]
        total = total + 2.0 * (g[0][1] * g[1][0] + g[0][2] * g[2][0] + g[1][2] * g[2][1])
        source = (alpha_reg * 0.25) * total
        w = [(alpha_reg * 0.5) * (c + n) for n in around]
        scale = 1.0 / (c + ((w[0] + w[1]) + (w[2] + w[3]) + (w[4] + w[5])))
        return [v * scale for v in w] + [source * scale]

    def coefficients(p):
        g = []
        for a in range(3):
            u = U[a, p]
            g.append([
                U[a, p + 1] - U[a, p - 1], up(u, 0) - down(u, 0), up(u, 1) - down(u, 1),
            ])
        c = INV[p]
        around = [INV[p + 1], INV[p - 1], up(c, 0), down(c, 0), up(c, 1), down(c, 1)]
        for n, v in enumerate(stencil_terms(g, c, around)):
            CO[n, p] = v

    def jacobi(co, c, xp, xm):
        out = co(6) + co(0) * xp + co(1) * xm
        out = out + (co(2) * up(c, 0) + co(3) * down(c, 0))
        return out + (co(4) * up(c, 1) + co(5) * down(c, 1))

    def main_sweep(step, planes):
        read, write = (SA, SB) if step % 2 == 0 else (SB, SA)
        for p in planes:
            write[p] = jacobi(lambda n: CO[n, p], read[p], read[p + 1], read[p - 1])

    early = [range(own0 + 1 + t, end - 1 - t) for t in range(SWEEPS)]
    near = jnp.logical_or(lane2 < REACH, lane2 >= nz - REACH)
    edge = jnp.logical_or(lane2 < SWEEPS, lane2 >= nz - SWEEPS)
    ends = jnp.logical_or(lane2 == 0, lane2 == nz - 1)

    def ring_next(a, b):
        ua, ub = up(a, 1, slot), up(b, 1, slot)
        cut = lane2 >= nz - slot
        return jnp.where(cut, ub, ua), jnp.where(cut, ua, ub)

    def ring_prev(a, b):
        da, db = down(a, 1, slot), down(b, 1, slot)
        cut = lane2 < slot
        return jnp.where(cut, db, da), jnp.where(cut, da, db)

    def joined(own, far):
        return jnp.where(lower2, far, own), jnp.where(lower2, own, far)

    def far_strip(sec, which, f):
        v = jnp.concatenate([ZR[sec, which, hf, f].astype(F32) for hf in (0, 1)], axis=0)
        return v * sg if f == 1 else v

    def outer_strips(sec):
        v = jnp.concatenate([ZO[sec, hf, 0].astype(F32) for hf in (0, 1)], axis=0)
        fields = [v] + [pltpu.roll(v, nz - moves[j], 1) for j in (1, 2, 3)]
        fields[1] = fields[1] * sg
        a, b = ZO[sec, 0, 1].astype(F32), ZO[sec, 1, 1].astype(F32)
        b = jnp.where(sec == 0, b, pltpu.roll(a, nz // 2, 1))
        return fields + [jnp.concatenate([a, b], axis=0)]

    def local_strip(f, planes):
        src = SA if f == SIG else QF.at[min(f, 4)]
        return strips([(at, src[p]) for at, p in planes], lane2)

    inside = [(k, own0 + k) for k in range(nx)]
    outside = [(0, end)] + [(nx - HALO + e, e) for e in range(HALO)]

    def section(sec, carry):
        arrived(sec, G_SIB, R.at[sec, :, :, 0:m])

        @pl.when(sec == 0)
        def _():
            for e in range(own0, end):
                take(0, e, (1,))

        @pl.when(sec == 1)
        def _():
            for e in range(sib0, end):
                take(1, e, (0, 1))

        for k in range(m):
            p = own0 + k
            c = [QF[f, p] for f in range(5)]
            ychange = line_flux(c, 1, 0)
            zchange = line_flux(c, 2, 1)
            for f in range(5):
                T[f, k] = ychange[f] + jnp.where(near, 0.0, zchange[f])
        h8, h7 = x_face(sib0 - 1), x_face(sib0 - 2)
        for f in range(5):
            T[f, m - 1] = T[f, m - 1] + (h8[f] - h7[f])
            T[f, m - 2] = T[f, m - 2] + h7[f]
        for p in range(own0, end):
            velocities(p)
        for p in early[0]:
            coefficients(p)
        WS[...] = local_strip(SIG, inside)
        for step in range(SWEEPS):
            main_sweep(step, early[step])

        arrived(sec, G_ZSAME, ZR.at[sec, 0])

        @pl.when(sec == 1)
        def _():
            arrived(sec, G_ZSIB, ZR.at[sec, 1, :, 0:EN])

        for f in (0, 1, 2, 3, EN):
            a = far_strip(sec, 0, f)
            if f != EN:
                a = jnp.where(first2, a, far_strip(sec, sec, f))
            WQ[min(f, 4), 0], WQ[min(f, 4), 1] = joined(local_strip(f, inside), a)
        lo = line_flux([WQ[f, 0] for f in range(5)], 2, 1)
        hi = line_flux([WQ[f, 1] for f in range(5)], 2, 1)
        for f in range(5):
            zb = jnp.where(lower2, hi[f], lo[f])
            for k in range(m):
                r = pltpu.roll(zb, nz - half - slot * k, 1)
                T[f, k] = T[f, k] + jnp.where(near, r, 0.0)

        arrived(sec, G_OUT, R.at[sec, :, 0:4, 0:HALO])
        arrived(sec, G_EN, R.at[sec, :, EN, 0:REACH])
        for e in range(HALO):
            take(sec, e, (0, 1), (0, 1, 2, 3, EN) if e >= HALO - REACH else range(4))
        faces = [x_face(p) for p in range(own0 - 1, sib0 - 2)]
        for f in range(5):
            for k in range(m - 2):
                T[f, k] = T[f, k] + (faces[k + 1][f] - faces[k][f])
            T[f, m - 2] = T[f, m - 2] - faces[m - 2][f]

        @pl.when(sec == 0)
        def _():
            advance(0)
            send_state(FIRST)

        for p in range(HALO):
            velocities(p)
        for p in range(1, own0 + 1):
            coefficients(p)

        arrived(sec, G_FAR, R.at[sec, :, 0:EN, 0:2])
        @pl.when(sec == 0)
        def _():
            arrived(0, G_ZOUT, ZO.at[0])

        @pl.when(sec == 1)
        def _():
            arrived(1, G_ZOUT, R.at[1, 0, 0, 0:3])

        for e in range(HALO):
            take(sec, e, (0, 1), (SIG,))
        take(sec, end, (0, 1), range(EN))
        velocities(end)
        coefficients(end - 1)
        outer_far = outer_strips(sec)
        for f in range(4):
            WQ[f, 2], WQ[f, 3] = joined(local_strip(f, outside), outer_far[f])
        for n in range(4):
            inv = 1.0 / WQ[0, n]
            WI[n] = inv
            for a in range(3):
                WU[a, n] = WQ[1 + a, n] * inv
        a = jnp.where(first2, far_strip(sec, 0, SIG), far_strip(sec, sec, SIG))
        w = list(joined(WS[...], a))
        w += joined(local_strip(SIG, outside), outer_far[SIG])

        for b in (0, 1):
            pair = (b, 2 + b)
            g = [[], []]
            for a in range(3):
                v = [WU[a, n] for n in pair]
                nxt, prv = ring_next(*v), ring_prev(*v)
                for i in (0, 1):
                    g[i].append([nxt[i] - prv[i], up(v[i], 0) - down(v[i], 0),
                                 up(v[i], 1) - down(v[i], 1)])
            c = [WI[n] for n in pair]
            nxt, prv = ring_next(*c), ring_prev(*c)
            for i in (0, 1):
                around = [nxt[i], prv[i], up(c[i], 0), down(c[i], 0), up(c[i], 1), down(c[i], 1)]
                for n, v in enumerate(stencil_terms(g[i], c[i], around)):
                    WC[n, pair[i]] = v

        for step in range(SWEEPS):
            main_sweep(step, [p for p in range(step + 1, np_ - 1 - step) if p not in early[step]])
            fresh = [None] * 4
            for b in (0, 1):
                pair = (b, 2 + b)
                v = [w[n] for n in pair]
                nxt, prv = ring_next(*v), ring_prev(*v)
                for i in (0, 1):
                    fresh[pair[i]] = jacobi(lambda n: WC[n, pair[i]], v[i], nxt[i], prv[i])
            w = fresh
        S = SA

        for g, planes in ((0, [(k, own0 + k) for k in range(m + 1)]), (1, [(nx - 1, own0 - 1)])):
            both = jnp.where(lower2, w[2 * g + 1], w[2 * g])
            for at, p in planes:
                S[p] = jnp.where(edge, pltpu.roll(both, nz - half - slot * at, 1), S[p])

        @pl.when(sec == 0)
        def _():
            advance(SIG)
            send_state(MIDDLE)

        diffs = []
        for n in (0, 1):
            v = w[n]
            e = v * WU[2, n]
            diffs.append((up(v, 1) - down(v, 1), up(e, 1) - down(e, 1)))
        for i in (0, 1):
            ZB[i] = jnp.where(lower2, diffs[1][i], diffs[0][i])

        for k in range(m):
            p = own0 + k
            shift = nz - half - slot * k
            xp, xm = S[p + 1], S[p - 1]
            T[1, k] = T[1, k] + 0.5 * (xp - xm)
            power = xp * U[0, p + 1] - xm * U[0, p - 1]
            s = S[p]
            T[2, k] = T[2, k] + 0.5 * (up(s, 0) - down(s, 0))
            e = s * U[1, p]
            power = power + (up(e, 0) - down(e, 0))
            T[3, k] = T[3, k] + 0.5 * jnp.where(
                ends, pltpu.roll(ZB[0], shift, 1), up(s, 1) - down(s, 1))
            e = s * U[2, p]
            power = power + jnp.where(ends, pltpu.roll(ZB[1], shift, 1), up(e, 1) - down(e, 1))
            T[4, k] = T[4, k] + 0.5 * power

        @pl.when(sec == 0)
        def _():
            for f in (1, 2, 3, EN):
                advance(f)
            send_state(LAST)
            order = list(range(m)) + list(range(m - 1, -1, -1))
            packs = []
            for f in range(6):
                src = S if f == SIG else QF.at[min(f, 4)]
                v = strips([(at, src[own0 + k]) for at, k in enumerate(order)], lane2)
                v = v * sg if f == 1 else v
                packs.append(v)
                v = v.astype(BF16)
                PKS[0, f], PKS[1, f] = v[near_rows], v[far_rows]
                if f != EN:
                    PKO[0, f], PKO[1, f] = v[far_rows], v[near_rows]
            v = corner(packs, lane2).astype(BF16)
            PKZ[0], PKZ[1] = v[far_rows], v[near_rows]
            v = packs[SIG]
            PKZ[2] = jnp.where(lane >= nz // 2, v[far_rows],
                               pltpu.roll(v[near_rows], nz // 2, 1)).astype(BF16)
            send_state(None)

        @pl.when(sec == 1)
        def _():
            for k in range(m):
                rk = k + h * (m - 1 - 2 * k)
                for f in range(5):
                    v = 0.5 * ((CI[f, k] - time_step * T[f, k]) + QF[f, own0 + k])
                    v = v * sg if f == 1 else v
                    new_out[f, block(k)] = v[near_rows]
                    FO[f, rk] = v[far_rows]
                s = S[own0 + k]
                ent_out[block(k)] = s[near_rows]
                FE[rk] = s[far_rows]
                if k in (m // 2 - 1, m - 1):
                    for c in result_copies(2 * k // m):
                        c.start()

        return carry

    lax.fori_loop(0, 2, section, 0)

    done = list(first)
    for fields in (FIRST, MIDDLE, LAST, None):
        done += second_sends(fields)
    for c in done:
        c.wait_send()
    for part in range(2):
        for c in result_copies(part):
            c.wait_send()
    for n, ref in ((0, FO), (1, FE)):
        pltpu.make_async_remote_copy(
            src_ref=ref, dst_ref=ref, send_sem=last_sem.at[0], recv_sem=last_sem.at[2 + n],
            device_id=(gx, 1 - h, gz), device_id_type=MESH,
        ).wait_recv()


def solution(mesh):
    counts = (mesh.shape["gx"], mesh.shape["gy"], mesh.shape["gz"])
    assert counts[1] == 2 and counts[2] == 2 and counts[0] > 2

    def step(conserved, sigma_prev):
        _, nx, ny, nz = conserved.shape
        m = nx // 2
        np_ = m + 2 * HALO
        wide = (2 * ny, nz)
        slot = nz // nx
        assert nx == 2 * m and m % 2 == 0 and HALO == m + 1 and SWEEPS % 2 == 0 and nx * slot == nz
        assert slot >= 4 * SWEEPS and slot & (slot - 1) == 0
        vmem = pl.BlockSpec(memory_space=pltpu.VMEM)
        tile = (ny, nz)
        return pl.pallas_call(
            functools.partial(kernel, counts),
            out_shape=(
                pltpu.VMEM((5, nx, ny, nz), F32),
                pltpu.VMEM((nx, ny, nz), F32),
            ),
            in_specs=[pl.BlockSpec(memory_space=pltpu.HBM)] * 2,
            out_specs=(vmem, vmem),
            scratch_shapes=[
                pltpu.VMEM((5, nx) + tile, BF16),
                pltpu.VMEM((nx,) + tile, F32),
                pltpu.VMEM((nx,) + tile, BF16),
                pltpu.VMEM((2, 6) + tile, BF16),
                pltpu.VMEM((2, 2) + tile, BF16),
                pltpu.VMEM((2, 2, 6, np_) + tile, BF16),
                pltpu.VMEM((2, 2, 2, 6) + tile, BF16),
                pltpu.VMEM((2, 2, 2) + tile, BF16),
                pltpu.VMEM((2, 6, m) + tile, BF16),
                pltpu.VMEM((2, 5, 2) + tile, BF16),
                pltpu.VMEM((2, 6) + tile, BF16),
                pltpu.VMEM((2, 5) + tile, BF16),
                pltpu.VMEM((3,) + tile, BF16),
                pltpu.VMEM((5, m) + tile, F32),
                pltpu.VMEM((m,) + tile, F32),
                pltpu.VMEM((5, np_) + wide, F32),
                pltpu.VMEM((5, m) + wide, F32),
                pltpu.VMEM((3, np_) + wide, F32),
                pltpu.VMEM((np_,) + wide, F32),
                pltpu.VMEM((7, np_) + wide, F32),
                pltpu.VMEM((np_,) + wide, F32),
                pltpu.VMEM((np_,) + wide, F32),
                pltpu.VMEM((5, 4) + wide, F32),
                pltpu.VMEM((3, 4) + wide, F32),
                pltpu.VMEM((4,) + wide, F32),
                pltpu.VMEM((7, 4) + wide, F32),
                pltpu.VMEM(wide, F32),
                pltpu.VMEM((2,) + wide, F32),
                pltpu.VMEM((5, m) + wide, F32),
                pltpu.SemaphoreType.DMA((2,)),
                pltpu.SemaphoreType.DMA((2, 7)),
                pltpu.SemaphoreType.DMA((4,)),
                pltpu.SemaphoreType.DMA((2,)),
            ],
            compiler_params=pltpu.CompilerParams(collective_id=0, has_side_effects=True),
        )(conserved, sigma_prev)

    return jax.shard_map(
        step,
        mesh=mesh,
        in_specs=(P(None, "gx", "gy", "gz"), P("gx", "gy", "gz")),
        out_specs=(P(None, "gx", "gy", "gz"), P("gx", "gy", "gz")),
        check_vma=False,
    )
```

```python
import functools

import jax
import jax.numpy as jnp
from jax import lax
from jax.experimental import pallas as pl
from jax.experimental.pallas import tpu as pltpu
from jax.sharding import PartitionSpec as P

SWEEPS = 4
HALO = SWEEPS + 1
REACH = 3
gamma_gas = 1.4
alpha_reg = 4.0
time_step = 0.08
MESH = pl.DeviceIdType.MESH
F32 = jnp.float32
BF16 = jnp.bfloat16

SIG, EN = 4, 5
FIRST, MIDDLE, LAST = (0, 1), (SIG, EN), (1, SIG)
G_SIB, G_OUT, G_FAR, G_ZSAME, G_ZSIB, G_ZOUT, G_EN = range(7)


def edges(c, p1, m1, p2, m2):
    even = (47.0 / 60.0) * c + (7.0 / 60.0) * (p1 + m1) - (0.5 / 60.0) * (p2 + m2)
    odd = (20.0 / 60.0) * (p1 - m1) - (2.5 / 60.0) * (p2 - m2)
    return even + odd, even - odd


def physical_flux(v, d):
    inv = 1.0 / v[0]
    u = [v[1] * inv, v[2] * inv, v[3] * inv]
    kinetic = 0.5 * (v[1] * u[0] + v[2] * u[1] + v[3] * u[2])
    p = (gamma_gas - 1.0) * (v[4] - kinetic)
    n = u[d]
    flux = [v[1 + d], v[1] * n, v[2] * n, v[3] * n, (v[4] + p) * n]
    flux[1 + d] = flux[1 + d] + p
    return flux, jnp.abs(n) + jnp.sqrt(gamma_gas * jnp.abs(p) * inv)


def face_flux(left, right, d):
    fl, sl = physical_flux(left, d)
    fr, sr = physical_flux(right, d)
    speed = jnp.maximum(sl, sr)
    return [0.5 * ((a + b) - speed * (r - l)) for a, b, l, r in zip(fl, fr, left, right)]


def up(v, axis, by=1):
    return pltpu.roll(v, (v.shape[axis] - by) % v.shape[axis], axis)


def down(v, axis, by=1):
    return pltpu.roll(v, by, axis)


def kernel(counts, cons_hbm, sigma_hbm, new_out, ent_out, cons, sigma, SGB, FP, FZ, R, ZR, ZO, STO, STS, PKS, PKO, PKZ,
           FO, FE,
           QF, CI, U, INV, CO, SA, SB, WQ, WU, WI, WC, WS, ZB, T, send_sem, recv_sem, last_sem, in_sem):
    loads = [pltpu.make_async_copy(cons_hbm, cons, in_sem.at[0]),
             pltpu.make_async_copy(sigma_hbm, sigma, in_sem.at[1])]
    for c in loads:
        c.start()
    gx, h, gz = lax.axis_index("gx"), lax.axis_index("gy"), lax.axis_index("gz")
    nx, ny, nz = sigma.shape
    m = nx // 2
    np_ = m + 2 * HALO
    own0, sib0, end = HALO, HALO + m, HALO + 2 * m
    slot = nz // nx
    half = slot // 2
    near_rows, far_rows = slice(0, ny), slice(ny, 2 * ny)
    sg = (1 - 2 * h).astype(F32)

    right, left = lax.rem(gx + 1, counts[0]), lax.rem(gx + counts[0] - 1, counts[0])
    outer = lax.rem(gx + counts[0] - 1 + 2 * h, counts[0])
    inner = lax.rem(gx + counts[0] + 1 - 2 * h, counts[0])
    oz = 1 - gz
    rows_of = (h * 0, h * 0 + 1)

    def frame(e):
        return e + h * (np_ - 1 - 2 * e)

    def block(k):
        return k + h * (nx - 1 - 2 * k)

    lane = lax.broadcasted_iota(jnp.int32, (ny, nz), 1)
    lane2 = lax.broadcasted_iota(jnp.int32, (2 * ny, nz), 1)
    lower2 = (lane2 & (slot - 1)) < half
    first2 = lane2 < nz // 2

    def strips(parts, lanes):
        acc = None
        for at, v in parts:
            r = pltpu.roll(v, (half + slot * at) % nz, 1)
            acc = r if acc is None else jnp.where(lanes >= slot * at, r, acc)
        return acc

    def descriptors(listed, which):
        made = []
        for sec, src, dst, group, where in listed:
            made.append(pltpu.make_async_remote_copy(
                src_ref=src, dst_ref=dst, send_sem=send_sem.at[which],
                recv_sem=recv_sem.at[sec, group], device_id=where, device_id_type=MESH,
            ))
        return made

    def arrived(sec, group, ref):
        pltpu.make_async_remote_copy(
            src_ref=ref, dst_ref=ref, send_sem=send_sem.at[0], recv_sem=recv_sem.at[sec, group],
            device_id=(gx, 1 - h, gz), device_id_type=MESH,
        ).wait_recv()

    barrier = pltpu.get_barrier_semaphore()
    peers = [(gx, 1 - h, gz), (outer, h, oz), (outer, 1 - h, oz)]
    peers += [(x, y, gz) for x in (right, left) for y in (h, 1 - h)]
    peers += [(gx, h, oz), (gx, 1 - h, oz)]
    for peer in peers:
        pl.semaphore_signal(barrier, inc=1, device_id=peer, device_id_type=MESH)

    for c in loads:
        c.wait()
    SGB[...] = sigma[...].astype(BF16)
    moves = (0, half, nz // 2, nz // 2 + half)

    def corner(v, lanes):
        cell = lanes & (slot - 1)
        middle = jnp.logical_and(cell >= half - SWEEPS, cell < half + SWEEPS)
        last = jnp.logical_and(lanes >= half - SWEEPS, lanes < nz // 2 + half - SWEEPS)
        r = [v[0]] + [pltpu.roll(v[j], moves[j], 1) for j in (1, 2, 3)]
        return jnp.where(middle, jnp.where(lanes >= nz // 2, r[0], r[2]),
                         jnp.where(last, r[3], r[1]))

    packed = [[], []]
    for f in range(6):
        for target in (0, 1):
            parts = []
            for k in range(nx):
                p = k if target == 0 else nx - 1 - k
                parts.append((k, sigma[p] if f == SIG else cons[min(f, 4), p].astype(F32)))
            v = strips(parts, lane)
            FP[target, f] = v.astype(BF16)
            packed[target].append(v)
    for target in (0, 1):
        FZ[target, 0] = corner(packed[target], lane).astype(BF16)
        FZ[target, 1] = packed[target][SIG].astype(BF16)
    pl.semaphore_wait(barrier, len(peers))

    def first_sends():
        listed = []

        def copy(*c):
            listed.append(c)

        odd = lax.rem(gx, 2)
        sides = []
        for side in (odd, 1 - odd):
            to = left + side * (right - left)
            hf = h * side + (1 - h) * (1 - side)
            sides.append((side, hf, (to, 1 - side, gz), (to, side, gz)))
        for side, hf, to, _ in sides:
            a, e = (nx - HALO) * side, sib0 * (1 - side)
            skip = (HALO - REACH) * side
            copy(0, cons.at[0:4, pl.ds(a, HALO)], R.at[0, hf, 0:4, pl.ds(e, HALO)], G_OUT, to)
            copy(0, cons.at[4, pl.ds(a + skip, REACH)], R.at[0, hf, EN, pl.ds(e + skip, REACH)],
                 G_EN, to)
        for target, hf in ((0, h), (1, 1 - h)):
            to = right if target == 0 else left
            copy(0, FZ.at[target], ZO.at[0, hf], G_ZOUT, (to, rows_of[target], oz))
        for side, hf, to, over in sides:
            a, e = (nx - HALO) * side, sib0 * (1 - side)
            copy(0, SGB.at[pl.ds(a, HALO)], R.at[0, hf, SIG, pl.ds(e, HALO)], G_FAR, to)
            a, e = (nx - 1) * side, (np_ - 1) * (1 - side)
            copy(0, cons.at[0:4, pl.ds(a, 1)], R.at[0, 1 - hf, 0:4, pl.ds(e, 1)], G_FAR, over)
            copy(0, SGB.at[pl.ds(a, 1)], R.at[0, 1 - hf, SIG, pl.ds(e, 1)], G_FAR, over)
        e = HALO - m + m * h
        sib = (gx, 1 - h, gz)
        copy(0, cons.at[0:4], R.at[0, 1, 0:4, pl.ds(e, nx)], G_SIB, sib)
        copy(0, SGB, R.at[0, 1, SIG, pl.ds(e, nx)], G_SIB, sib)
        copy(0, cons.at[4], R.at[0, 1, EN, pl.ds(e, nx)], G_SIB, sib)

        for target, hf in ((0, h), (1, 1 - h)):
            copy(0, FP.at[target], ZR.at[0, 0, hf], G_ZSAME, (gx, rows_of[target], oz))
        return descriptors(listed, 0)

    def second_sends(fields):
        listed = []

        def copy(*c):
            listed.append((1,) + c)

        back = sib0 - 2 * m * h
        over = HALO - m + 2 * m * h
        sib, across = (gx, 1 - h, gz), (outer, 1 - h, gz)
        if fields is not None:
            a, b = fields
            group = G_FAR if fields == MIDDLE else G_OUT
            copy(STO.at[:, a:b], R.at[1, :, a:b, pl.ds(back, m)], group, across)
            copy(STS.at[:, a:b, 1:2], R.at[1, :, a:b, pl.ds((np_ - 1) * h, 1)], group,
                 (inner, h, gz))
            copy(STS.at[:, a:b, 0:1], R.at[1, :, a:b, pl.ds((np_ - 1) * (1 - h), 1)], G_FAR,
                 (outer, h, gz))
            if fields == LAST:
                copy(STO.at[:, EN, pl.ds(h, REACH)], R.at[1, :, EN, pl.ds(back + h, REACH)], G_EN,
                     across)
                copy(STO.at[:, EN], R.at[1, :, EN, pl.ds(over, m)], G_SIB, sib)
            copy(STO.at[:, a:b], R.at[1, :, a:b, pl.ds(over, m)], G_SIB, sib)
        else:
            copy(PKS, ZR.at[1, 0], G_ZSAME, (gx, h, oz))
            copy(PKO, ZR.at[1, 1, :, 0:EN], G_ZSIB, (gx, 1 - h, oz))
            copy(PKZ.at[0:2], ZO.at[1, :, 0], G_ZOUT, (outer, 1 - h, oz))
            copy(PKZ.at[2], ZO.at[1, 0, 1], G_ZOUT, (outer, 1 - h, oz))
        return descriptors(listed, 1)

    def send_state(fields):
        for c in second_sends(fields):
            c.start()

    def advance(f):
        for k in range(m):
            rk = k + h * (m - 1 - 2 * k)
            if f == SIG:
                state = SA[own0 + k].astype(BF16)
            else:
                q = min(f, 4)
                initial = QF[q, own0 + k]
                CI[q, k] = initial
                state = (initial - time_step * T[q, k]).astype(BF16)
                QF[q, own0 + k] = state.astype(F32)
                if f == 1:
                    state = (state.astype(F32) * sg).astype(BF16)
            STO[0, f, rk], STO[1, f, rk] = state[far_rows], state[near_rows]
            if f != EN and k in (0, m - 1):
                at = 0 if k == 0 else 1
                STS[0, f, at], STS[1, f, at] = state[near_rows], state[far_rows]

    first = first_sends()
    for c in first:
        c.start()

    for k in range(nx):
        p = block(k)
        for f in range(5):
            v = cons.at[f][p].astype(F32)
            QF[f, own0 + k, near_rows] = v * sg if f == 1 else v
        SA[own0 + k, near_rows] = sigma[p]

    def result_copies(part):
        mh = m // 2
        a = mh * (part + h - 2 * part * h)
        return [pltpu.make_async_remote_copy(
            src_ref=src, dst_ref=dst, send_sem=last_sem.at[n], recv_sem=last_sem.at[2 + n],
            device_id=(gx, 1 - h, gz), device_id_type=MESH,
        ) for n, (src, dst) in enumerate((
            (FO.at[:, pl.ds(a, mh)], new_out.at[:, pl.ds(m * h + a, mh)]),
            (FE.at[pl.ds(a, mh)], ent_out.at[pl.ds(m * h + a, mh)])))]

    def take(sec, e, halves, fields=range(6)):
        for hf in halves:
            rows = far_rows if hf else near_rows
            for f in fields:
                v = R[sec, hf, f, frame(e)].astype(F32)
                if f == SIG:
                    SA[e, rows] = v
                else:
                    QF[min(f, 4), e, rows] = v * sg if f == 1 else v

    def line_flux(fields, d, axis):
        lefts, rights = [], []
        for c in fields:
            l, r = edges(c, up(c, axis), down(c, axis), up(c, axis, 2), down(c, axis, 2))
            lefts.append(l)
            rights.append(up(r, axis))
        return [v - down(v, axis) for v in face_flux(lefts, rights, d)]

    def x_face(p):
        lefts, rights = [], []
        for f in range(5):
            v = [QF[f, p + o] for o in range(-2, 4)]
            lefts.append(edges(v[2], v[3], v[1], v[4], v[0])[0])
            rights.append(edges(v[3], v[4], v[2], v[5], v[1])[1])
        return face_flux(lefts, rights, 0)

    def velocities(p):
        inv = 1.0 / QF[0, p]
        INV[p] = inv
        for a in range(3):
            U[a, p] = QF[1 + a, p] * inv

    def stencil_terms(g, c, around):
        div = g[0][0] + g[1][1] + g[2][2]
        total = div * div + g[0][0] * g[0][0] + g[1][1] * g[1][1] + g[2][2] * g[2][2]
        total = total + 2.0 * (g[0][1] * g[1][0] + g[0][2] * g[2][0] + g[1][2] * g[2][1])
        source = (alpha_reg * 0.25) * total
        w = [(alpha_reg * 0.5) * (c + n) for n in around]
        scale = 1.0 / (c + ((w[0] + w[1]) + (w[2] + w[3]) + (w[4] + w[5])))
        return [v * scale for v in w] + [source * scale]

    def coefficients(p):
        g = []
        for a in range(3):
            u = U[a, p]
            g.append([
                U[a, p + 1] - U[a, p - 1], up(u, 0) - down(u, 0), up(u, 1) - down(u, 1),
            ])
        c = INV[p]
        around = [INV[p + 1], INV[p - 1], up(c, 0), down(c, 0), up(c, 1), down(c, 1)]
        for n, v in enumerate(stencil_terms(g, c, around)):
            CO[n, p] = v

    def jacobi(co, c, xp, xm):
        out = co(6) + (co(2) * up(c, 0) + co(3) * down(c, 0))
        return out + ((co(0) * xp + co(1) * xm) + (co(4) * up(c, 1) + co(5) * down(c, 1)))

    def main_sweep(step, planes):
        read, write = (SA, SB) if step % 2 == 0 else (SB, SA)
        for p in planes:
            write[p] = jacobi(lambda n: CO[n, p], read[p], read[p + 1], read[p - 1])

    early = [range(own0 + 1 + t, end - 1 - t) for t in range(SWEEPS)]
    near = jnp.logical_or(lane2 < REACH, lane2 >= nz - REACH)
    edge = jnp.logical_or(lane2 < SWEEPS, lane2 >= nz - SWEEPS)
    ends = jnp.logical_or(lane2 == 0, lane2 == nz - 1)

    def ring_next(a, b):
        ua, ub = up(a, 1, slot), up(b, 1, slot)
        cut = lane2 >= nz - slot
        return jnp.where(cut, ub, ua), jnp.where(cut, ua, ub)

    def ring_prev(a, b):
        da, db = down(a, 1, slot), down(b, 1, slot)
        cut = lane2 < slot
        return jnp.where(cut, db, da), jnp.where(cut, da, db)

    def joined(own, far):
        return jnp.where(lower2, far, own), jnp.where(lower2, own, far)

    def far_strip(sec, which, f):
        v = jnp.concatenate([ZR[sec, which, hf, f].astype(F32) for hf in (0, 1)], axis=0)
        return v * sg if f == 1 else v

    def outer_strips(sec):
        v = jnp.concatenate([ZO[sec, hf, 0].astype(F32) for hf in (0, 1)], axis=0)
        fields = [v] + [pltpu.roll(v, nz - moves[j], 1) for j in (1, 2, 3)]
        fields[1] = fields[1] * sg
        a, b = ZO[sec, 0, 1].astype(F32), ZO[sec, 1, 1].astype(F32)
        b = jnp.where(sec == 0, b, pltpu.roll(a, nz // 2, 1))
        return fields + [jnp.concatenate([a, b], axis=0)]

    def local_strip(f, planes):
        src = SA if f == SIG else QF.at[min(f, 4)]
        return strips([(at, src[p]) for at, p in planes], lane2)

    inside = [(k, own0 + k) for k in range(nx)]
    outside = [(0, end)] + [(nx - HALO + e, e) for e in range(HALO)]

    def section(sec, carry):
        arrived(sec, G_SIB, R.at[sec, :, :, 0:m])

        @pl.when(sec == 0)
        def _():
            for e in range(own0, end):
                take(0, e, (1,))

        @pl.when(sec == 1)
        def _():
            for e in range(sib0, end):
                take(1, e, (0, 1))

        for k in range(m):
            p = own0 + k
            c = [QF[f, p] for f in range(5)]
            ychange = line_flux(c, 1, 0)
            zchange = line_flux(c, 2, 1)
            for f in range(5):
                T[f, k] = ychange[f] + jnp.where(near, 0.0, zchange[f])
        h8, h7 = x_face(sib0 - 1), x_face(sib0 - 2)
        for f in range(5):
            T[f, m - 1] = T[f, m - 1] + (h8[f] - h7[f])
            T[f, m - 2] = T[f, m - 2] + h7[f]
        for p in range(own0, end):
            velocities(p)
        for p in early[0]:
            coefficients(p)
        WS[...] = local_strip(SIG, inside)
        for step in range(SWEEPS):
            main_sweep(step, early[step])

        arrived(sec, G_ZSAME, ZR.at[sec, 0])

        @pl.when(sec == 1)
        def _():
            arrived(sec, G_ZSIB, ZR.at[sec, 1, :, 0:EN])

        for f in (0, 1, 2, 3, EN):
            a = far_strip(sec, 0, f)
            if f != EN:
                a = jnp.where(first2, a, far_strip(sec, sec, f))
            WQ[min(f, 4), 0], WQ[min(f, 4), 1] = joined(local_strip(f, inside), a)
        lo = line_flux([WQ[f, 0] for f in range(5)], 2, 1)
        hi = line_flux([WQ[f, 1] for f in range(5)], 2, 1)
        for f in range(5):
            zb = jnp.where(lower2, hi[f], lo[f])
            for k in range(m):
                r = pltpu.roll(zb, nz - half - slot * k, 1)
                T[f, k] = T[f, k] + jnp.where(near, r, 0.0)

        arrived(sec, G_OUT, R.at[sec, :, 0:4, 0:HALO])
        arrived(sec, G_EN, R.at[sec, :, EN, 0:REACH])
        for e in range(HALO):
            take(sec, e, (0, 1), (0, 1, 2, 3, EN) if e >= HALO - REACH else range(4))
        faces = [x_face(p) for p in range(own0 - 1, sib0 - 2)]
        for f in range(5):
            for k in range(m - 2):
                T[f, k] = T[f, k] + (faces[k + 1][f] - faces[k][f])
            T[f, m - 2] = T[f, m - 2] - faces[m - 2][f]

        @pl.when(sec == 0)
        def _():
            advance(0)
            send_state(FIRST)

        for p in range(HALO):
            velocities(p)
        for p in range(1, own0 + 1):
            coefficients(p)

        arrived(sec, G_FAR, R.at[sec, :, 0:EN, 0:2])
        @pl.when(sec == 0)
        def _():
            arrived(0, G_ZOUT, ZO.at[0])

        @pl.when(sec == 1)
        def _():
            arrived(1, G_ZOUT, R.at[1, 0, 0, 0:3])

        for e in range(HALO):
            take(sec, e, (0, 1), (SIG,))
        take(sec, end, (0, 1), range(EN))
        velocities(end)
        coefficients(end - 1)
        outer_far = outer_strips(sec)
        for f in range(4):
            WQ[f, 2], WQ[f, 3] = joined(local_strip(f, outside), outer_far[f])
        for n in range(4):
            inv = 1.0 / WQ[0, n]
            WI[n] = inv
            for a in range(3):
                WU[a, n] = WQ[1 + a, n] * inv
        a = jnp.where(first2, far_strip(sec, 0, SIG), far_strip(sec, sec, SIG))
        w = list(joined(WS[...], a))
        w += joined(local_strip(SIG, outside), outer_far[SIG])

        for b in (0, 1):
            pair = (b, 2 + b)
            g = [[], []]
            for a in range(3):
                v = [WU[a, n] for n in pair]
                nxt, prv = ring_next(*v), ring_prev(*v)
                for i in (0, 1):
                    g[i].append([nxt[i] - prv[i], up(v[i], 0) - down(v[i], 0),
                                 up(v[i], 1) - down(v[i], 1)])
            c = [WI[n] for n in pair]
            nxt, prv = ring_next(*c), ring_prev(*c)
            for i in (0, 1):
                around = [nxt[i], prv[i], up(c[i], 0), down(c[i], 0), up(c[i], 1), down(c[i], 1)]
                for n, v in enumerate(stencil_terms(g[i], c[i], around)):
                    WC[n, pair[i]] = v

        for step in range(SWEEPS):
            main_sweep(step, [p for p in range(step + 1, np_ - 1 - step) if p not in early[step]])
            fresh = [None] * 4
            for b in (0, 1):
                pair = (b, 2 + b)
                v = [w[n] for n in pair]
                nxt, prv = ring_next(*v), ring_prev(*v)
                for i in (0, 1):
                    fresh[pair[i]] = jacobi(lambda n: WC[n, pair[i]], v[i], nxt[i], prv[i])
            w = fresh
        S = SA

        for g, planes in ((0, [(k, own0 + k) for k in range(m + 1)]), (1, [(nx - 1, own0 - 1)])):
            both = jnp.where(lower2, w[2 * g + 1], w[2 * g])
            for at, p in planes:
                S[p] = jnp.where(edge, pltpu.roll(both, nz - half - slot * at, 1), S[p])

        @pl.when(sec == 0)
        def _():
            advance(SIG)
            send_state(MIDDLE)

        diffs = []
        for n in (0, 1):
            v = w[n]
            e = v * WU[2, n]
            diffs.append((up(v, 1) - down(v, 1), up(e, 1) - down(e, 1)))
        for i in (0, 1):
            ZB[i] = jnp.where(lower2, diffs[1][i], diffs[0][i])

        for k in range(m):
            p = own0 + k
            shift = nz - half - slot * k
            xp, xm = S[p + 1], S[p - 1]
            T[1, k] = T[1, k] + 0.5 * (xp - xm)
            power = xp * U[0, p + 1] - xm * U[0, p - 1]
            s = S[p]
            T[2, k] = T[2, k] + 0.5 * (up(s, 0) - down(s, 0))
            e = s * U[1, p]
            power = power + (up(e, 0) - down(e, 0))
            T[3, k] = T[3, k] + 0.5 * jnp.where(
                ends, pltpu.roll(ZB[0], shift, 1), up(s, 1) - down(s, 1))
            e = s * U[2, p]
            power = power + jnp.where(ends, pltpu.roll(ZB[1], shift, 1), up(e, 1) - down(e, 1))
            T[4, k] = T[4, k] + 0.5 * power

        @pl.when(sec == 0)
        def _():
            for f in (1, 2, 3, EN):
                advance(f)
            send_state(LAST)
            order = list(range(m)) + list(range(m - 1, -1, -1))
            packs = []
            for f in range(6):
                src = S if f == SIG else QF.at[min(f, 4)]
                v = strips([(at, src[own0 + k]) for at, k in enumerate(order)], lane2)
                v = v * sg if f == 1 else v
                packs.append(v)
                v = v.astype(BF16)
                PKS[0, f], PKS[1, f] = v[near_rows], v[far_rows]
                if f != EN:
                    PKO[0, f], PKO[1, f] = v[far_rows], v[near_rows]
            v = corner(packs, lane2).astype(BF16)
            PKZ[0], PKZ[1] = v[far_rows], v[near_rows]
            v = packs[SIG]
            PKZ[2] = jnp.where(lane >= nz // 2, v[far_rows],
                               pltpu.roll(v[near_rows], nz // 2, 1)).astype(BF16)
            send_state(None)

        @pl.when(sec == 1)
        def _():
            def result(f, k, rows):
                v = 0.5 * ((CI[f, k, rows] - time_step * T[f, k, rows]) + QF[f, own0 + k, rows])
                return v * sg if f == 1 else v

            for k in range(m):
                rk = k + h * (m - 1 - 2 * k)
                for f in range(5):
                    FO[f, rk] = result(f, k, far_rows)
                FE[rk] = S[own0 + k, far_rows]
                if k in (m // 2 - 1, m - 1):
                    for c in result_copies(2 * k // m):
                        c.start()
            for k in range(m):
                for f in range(5):
                    new_out[f, block(k)] = result(f, k, near_rows)
                ent_out[block(k)] = S[own0 + k, near_rows]

        return carry

    lax.fori_loop(0, 2, section, 0)

    done = list(first)
    for fields in (FIRST, MIDDLE, LAST, None):
        done += second_sends(fields)
    for c in done:
        c.wait_send()
    for part in range(2):
        for c in result_copies(part):
            c.wait_send()
    for n, ref in ((0, FO), (1, FE)):
        pltpu.make_async_remote_copy(
            src_ref=ref, dst_ref=ref, send_sem=last_sem.at[0], recv_sem=last_sem.at[2 + n],
            device_id=(gx, 1 - h, gz), device_id_type=MESH,
        ).wait_recv()


def solution(mesh):
    counts = (mesh.shape["gx"], mesh.shape["gy"], mesh.shape["gz"])
    assert counts[1] == 2 and counts[2] == 2 and counts[0] > 2

    def step(conserved, sigma_prev):
        _, nx, ny, nz = conserved.shape
        m = nx // 2
        np_ = m + 2 * HALO
        wide = (2 * ny, nz)
        slot = nz // nx
        assert nx == 2 * m and m % 2 == 0 and HALO == m + 1 and SWEEPS % 2 == 0 and nx * slot == nz
        assert slot >= 4 * SWEEPS and slot & (slot - 1) == 0
        vmem = pl.BlockSpec(memory_space=pltpu.VMEM)
        tile = (ny, nz)
        return pl.pallas_call(
            functools.partial(kernel, counts),
            out_shape=(
                pltpu.VMEM((5, nx, ny, nz), F32),
                pltpu.VMEM((nx, ny, nz), F32),
            ),
            in_specs=[pl.BlockSpec(memory_space=pltpu.HBM)] * 2,
            out_specs=(vmem, vmem),
            scratch_shapes=[
                pltpu.VMEM((5, nx) + tile, BF16),
                pltpu.VMEM((nx,) + tile, F32),
                pltpu.VMEM((nx,) + tile, BF16),
                pltpu.VMEM((2, 6) + tile, BF16),
                pltpu.VMEM((2, 2) + tile, BF16),
                pltpu.VMEM((2, 2, 6, np_) + tile, BF16),
                pltpu.VMEM((2, 2, 2, 6) + tile, BF16),
                pltpu.VMEM((2, 2, 2) + tile, BF16),
                pltpu.VMEM((2, 6, m) + tile, BF16),
                pltpu.VMEM((2, 5, 2) + tile, BF16),
                pltpu.VMEM((2, 6) + tile, BF16),
                pltpu.VMEM((2, 5) + tile, BF16),
                pltpu.VMEM((3,) + tile, BF16),
                pltpu.VMEM((5, m) + tile, F32),
                pltpu.VMEM((m,) + tile, F32),
                pltpu.VMEM((5, np_) + wide, F32),
                pltpu.VMEM((5, m) + wide, F32),
                pltpu.VMEM((3, np_) + wide, F32),
                pltpu.VMEM((np_,) + wide, F32),
                pltpu.VMEM((7, np_) + wide, F32),
                pltpu.VMEM((np_,) + wide, F32),
                pltpu.VMEM((np_,) + wide, F32),
                pltpu.VMEM((5, 4) + wide, F32),
                pltpu.VMEM((3, 4) + wide, F32),
                pltpu.VMEM((4,) + wide, F32),
                pltpu.VMEM((7, 4) + wide, F32),
                pltpu.VMEM(wide, F32),
                pltpu.VMEM((2,) + wide, F32),
                pltpu.VMEM((5, m) + wide, F32),
                pltpu.SemaphoreType.DMA((2,)),
                pltpu.SemaphoreType.DMA((2, 7)),
                pltpu.SemaphoreType.DMA((4,)),
                pltpu.SemaphoreType.DMA((2,)),
            ],
            compiler_params=pltpu.CompilerParams(collective_id=0, has_side_effects=True),
        )(conserved, sigma_prev)

    return jax.shard_map(
        step,
        mesh=mesh,
        in_specs=(P(None, "gx", "gy", "gz"), P("gx", "gy", "gz")),
        out_specs=(P(None, "gx", "gy", "gz"), P("gx", "gy", "gz")),
        check_vma=False,
    )
```
